256 devices in a mesh: slab: 128 (over x, y, z), rhs: 2 (over core).
Axes of the slice: x: 4, y: 4, z: 8, core: 2. Of those that a mesh axis runs over, the one named last changes fastest.
Arguments:
- bond_factor: float32 [128, 2, 256, 256], P('slab'), may hold values from -1 to 2
- tile_mask: int32 [128, 4, 4], P('slab'), may hold values from 0 to 1, as said below
- potential: float32 [128, 256], P('slab'), may hold values from 0.001 to 0.01
- injection: float32 [128, 2, 256, 128], P('slab', None, None, 'rhs'), may hold values from -0.125 to 0.125
Outputs:
- amplitude: float32 [128, 2, 256, 128], P('slab', None, None, 'rhs')
The draws below stay inside these ranges and needn't reach their ends.
Inputs may be any that keep to these rules, and one draw needn't show every extreme that they name: `tile_mask`: tiles on the diagonal of each slab's tile pattern are 1.
All inputs are finite; a program needn't handle non-finite values.
Results may differ from the reference program's by a relative error of at most 0.0003.
Values sent between devices are 32-bit elements; how exact they have to be, the bound alone decides.
A program may use at most 128 MiB of HBM per device.

```python
import math
import jax
import jax.numpy as jnp
from jax import lax

M = 256
TILE = 64
N = 128
R = 128


def draw_bond_factor(key, part):
    spread = 0.2 / math.sqrt(M)
    eye_real = jnp.eye(M, dtype=jnp.float32)
    noise_part = jax.random.truncated_normal(jax.random.fold_in(key, 13), -4.0, 4.0, (N, 2, M, M), jnp.float32)
    base_plane = jnp.stack([eye_real, jnp.zeros_like(eye_real)])
    return (base_plane[None] + spread * noise_part).astype(jnp.float32)


def draw_tile_mask(key, part):
    blocks = M // TILE
    coin_draw = jax.random.randint(jax.random.fold_in(key, 21), (N, blocks, blocks), 0, 4)
    present_tiles = jnp.where(coin_draw > 0, 1, 0).astype(jnp.int32)
    diagonal = jnp.eye(blocks, dtype=jnp.int32)[None]
    return jnp.maximum(present_tiles, diagonal).astype(jnp.int32)


def block_levels(key, extent, cuts, least, high):
    gain = 1.0
    for position, blocks in cuts:
        steps = jax.random.uniform(jax.random.fold_in(jax.random.fold_in(key, 6), position), (blocks,), jnp.float32, least / len(cuts), high / len(cuts))
        gain = gain * jnp.repeat(jnp.exp(steps), extent[position] // blocks).reshape((-1,) + (1,) * (len(extent) - 1 - position))
    return gain


def scatter_about(own_key, dims, deviation, most, split=(), kind=jnp.bfloat16):
    values = deviation * jax.random.normal(own_key, dims, jnp.float32)
    if split:
        values = values * block_levels(own_key, dims, split, -0.22, 0.18)
    return jnp.clip(values, -most, most).astype(kind)


def setup_inputs(seed: int = 0) -> dict:
    seeds = jax.random.split(jax.random.key(seed), 5)
    bond_factor = draw_bond_factor(jax.random.fold_in(seeds[4], 71), 0)
    tile_mask = draw_tile_mask(jax.random.fold_in(seeds[4], 71), 0)
    potential = jnp.clip(jnp.exp(math.log(0.01) - 2.30258502 * jax.random.uniform(seeds[2], (N, M), jnp.float32) ** block_levels(seeds[2], (N, M), ((0, 128),), -0.2, 0.2)), 0.001, 0.01)
    injection = scatter_about(seeds[3], (N, 2, M, R), 0.02, 0.125, ((0, 128), (3, 2)), jnp.float32)
    return {"bond_factor": bond_factor, "tile_mask": tile_mask, "potential": potential, "injection": injection}


PRECISE = lax.Precision.HIGHEST

def matmul_exact(operand, other):
    return jnp.dot(operand, other, precision=PRECISE)

def complex_product(operand, other):
    real_part = matmul_exact(operand[0], other[0]) - matmul_exact(operand[1], other[1])
    imag_part = matmul_exact(operand[0], other[1]) + matmul_exact(operand[1], other[0])
    return jnp.stack([real_part, imag_part])

def adjoint(operand):
    return jnp.stack([operand[0].T, -operand[1].T])

def real_form(matrix):
    return jnp.block([[matrix[0], -matrix[1]], [matrix[1], matrix[0]]])

def solve_stacked(factor_low, stacked):
    forward_part = lax.linalg.triangular_solve(factor_low, stacked, left_side=True, lower=True)
    return lax.linalg.triangular_solve(factor_low, forward_part, left_side=True, lower=True, transpose_a=True)

def complex_solve(matrix, sources):
    orbitals = matrix.shape[1]
    factor_low = jnp.linalg.cholesky(real_form(matrix))
    stacked = jnp.concatenate([sources[0], sources[1]], 0)
    solved = solve_stacked(factor_low, stacked)
    return jnp.stack([solved[:orbitals], solved[orbitals:]])

def reference(bond_factor, tile_mask, potential, injection):
    slab_count = bond_factor.shape[0]
    orbitals = bond_factor.shape[2]
    tile_size = orbitals // tile_mask.shape[2]

    def bond_of(pair):
        factor, pattern = pair
        expanded = jnp.repeat(jnp.repeat(pattern, tile_size, 0), tile_size, 1).astype(factor.dtype)
        masked = factor * expanded[None]
        return complex_product(masked, adjoint(masked))
    bonds = lax.map(bond_of, (bond_factor, tile_mask))
    previous = jnp.concatenate([jnp.zeros_like(bonds[:1]), bonds[:-1]], 0)
    at_end = jnp.arange(slab_count) == slab_count - 1

    def forward(state_pair, inputs):
        spike_prev, reduced_prev = state_pair
        bond_matrix, prior, energies, sources, final_slab = inputs
        coupling_down = -prior
        coupling_up = jnp.where(final_slab, jnp.zeros_like(bond_matrix), -bond_matrix)
        onsite = jnp.stack([jnp.diag(energies), jnp.zeros_like(bond_matrix[0])])
        schur = onsite + bond_matrix + prior - complex_product(coupling_down, spike_prev)
        reduced = sources - complex_product(coupling_down, reduced_prev)
        solved = complex_solve(schur, jnp.concatenate([coupling_up, reduced], 2))
        spike_next = solved[:, :, :orbitals]
        reduced_next = solved[:, :, orbitals:]
        return ((spike_next, reduced_next), (spike_next, reduced_next))
    start = (jnp.zeros_like(bonds[0]), jnp.zeros_like(injection[0]))
    final_state, (spikes, reduced_all) = lax.scan(forward, start, (bonds, previous, potential, injection, at_end))

    def backward(next_amplitude, inputs):
        spike, reduced = inputs
        current = reduced - complex_product(spike, next_amplitude)
        return (current, current)
    first_amplitude, amplitude = lax.scan(backward, jnp.zeros_like(injection[0]), (spikes, reduced_all), reverse=True)
    return amplitude
```

```python
import functools

import jax
import jax.numpy as jnp
from jax import lax
from jax.experimental import pallas as pl
from jax.experimental.pallas import tpu as pltpu
from jax.sharding import PartitionSpec as P

PRECISE = lax.Precision.HIGHEST
MESH = pl.DeviceIdType.MESH
F32 = jnp.float32
BF16 = jnp.bfloat16
RESIDUAL_LIMIT = 4.0e-4


def passed_along(array, axis, by):
    length = lax.axis_size(axis)
    pairs = [(i, i + by) for i in range(length) if 0 <= i + by < length]
    return lax.ppermute(array, axis, pairs)


def matmul_exact(operand, other):
    return jnp.dot(operand, other, precision=PRECISE)


def transposed_product(operand, other):
    return lax.dot_general(operand, other, (((0,), (0,)), ((), ())), precision=PRECISE)


def complex_product(operand, other):
    real_part = matmul_exact(operand[0], other[0]) - matmul_exact(operand[1], other[1])
    imag_part = matmul_exact(operand[0], other[1]) + matmul_exact(operand[1], other[0])
    return jnp.stack([real_part, imag_part])


def adjoint_product(operand, other):
    real_part = transposed_product(operand[0], other[0]) + transposed_product(operand[1], other[1])
    imag_part = transposed_product(operand[0], other[1]) - transposed_product(operand[1], other[0])
    return jnp.stack([real_part, imag_part])


def adjoint(operand):
    return jnp.stack([operand[0].T, -operand[1].T])


def real_form(matrix):
    return jnp.block([[matrix[0], -matrix[1]], [matrix[1], matrix[0]]])


def solve_stacked(factor_low, stacked):
    forward_part = lax.linalg.triangular_solve(factor_low, stacked, left_side=True, lower=True)
    return lax.linalg.triangular_solve(
        factor_low, forward_part, left_side=True, lower=True, transpose_a=True
    )


def direct_path(bond_factor, tile_mask, potential, injection):
    orbitals = bond_factor.shape[2]
    tile_size = orbitals // tile_mask.shape[2]
    slab_total = lax.axis_size("slab")
    position = lax.axis_index("slab")
    core_total = lax.axis_size("rhs")
    core_index = lax.axis_index("rhs")
    half_cols = orbitals // core_total
    pattern = jnp.repeat(jnp.repeat(tile_mask[0], tile_size, 0), tile_size, 1).astype(
        bond_factor.dtype
    )
    factor = bond_factor[0] * pattern[None]
    bond_matrix = complex_product(factor, adjoint(factor))
    previous = passed_along(bond_matrix, "slab", 1)
    onsite = jnp.stack([jnp.diag(potential[0]), jnp.zeros((orbitals, orbitals), potential.dtype)])
    matrix = onsite + bond_matrix + previous
    coupling_up = jnp.where(position == slab_total - 1, jnp.zeros_like(bond_matrix), -bond_matrix)
    coupling_down = -previous
    sources = injection[0]

    def apply_inverse(block, right_side):
        factor_low = jnp.linalg.cholesky(real_form(block))
        stacked = jnp.concatenate([right_side[0], right_side[1]], 0)
        solved = solve_stacked(factor_low, stacked)
        return jnp.stack([solved[:orbitals], solved[orbitals:]])

    def own_columns(block):
        return lax.dynamic_slice_in_dim(block, core_index * half_cols, half_cols, 2)

    levels = slab_total.bit_length() - 1
    for rank_bit in range(levels):
        stride = 1 << rank_bit
        spikes = apply_inverse(
            matrix,
            jnp.concatenate([own_columns(coupling_up), own_columns(coupling_down), sources], 2),
        )
        spike_up = spikes[:, :, :half_cols]
        spike_down = spikes[:, :, half_cols : 2 * half_cols]
        spike_waves = spikes[:, :, 2 * half_cols :]
        toward_upper = adjoint_product(
            coupling_down, jnp.concatenate([spike_down, spike_up, spike_waves], 2)
        )
        from_upper = passed_along(toward_upper, "slab", -stride)
        cross_part = toward_upper[:, :, half_cols : 2 * half_cols]
        toward_lower = adjoint_product(coupling_up, jnp.concatenate([spike_up, spike_waves], 2))
        outgoing = jnp.concatenate(
            [toward_lower[:, :, :half_cols], cross_part, toward_lower[:, :, half_cols:]], 2
        )
        from_lower = passed_along(outgoing, "slab", stride)
        diag_change = from_upper[:, :, :half_cols] + from_lower[:, :, :half_cols]
        new_up = -from_upper[:, :, half_cols : 2 * half_cols]
        coupling_new = from_lower[:, :, half_cols : 2 * half_cols]
        sources = sources - from_upper[:, :, 2 * half_cols :] - from_lower[:, :, 2 * half_cols :]
        gathered = (
            lax.all_gather(diag_change, "rhs", axis=2, tiled=True),
            lax.all_gather(new_up, "rhs", axis=2, tiled=True),
            lax.all_gather(coupling_new, "rhs", axis=2, tiled=True),
        )
        matrix = matrix - gathered[0]
        coupling_up = gathered[1]
        coupling_down = -adjoint(gathered[2])
    amplitude = apply_inverse(matrix, sources)
    return amplitude[None]


def split(value):
    high = value.astype(BF16)
    low = (value - high.astype(F32)).astype(BF16)
    return high, low


def dot(left, right):
    return jnp.dot(left, right, preferred_element_type=F32)


def dot3(left, right):
    high = dot(left[0], right[0])
    return high + (dot(left[0], right[1]) + dot(left[1], right[0]))


def pair_map(function, pair):
    return function(pair[0]), function(pair[1])


def tree_kernel(
    slabs,
    factor_ref,
    mask_ref,
    potential_ref,
    injection_ref,
    out_ref,
    flag_ref,
    ground,
    coupling,
    waves,
    flag,
    bond_out,
    near_bond,
    near_out,
    far_out,
    terms_in,
    wave_in,
    wave_out,
    back,
    send_sem,
    bond_sem,
    terms_sem,
    wave_sem,
    wave_send_sem,
    join_send_sem,
    join_sem,
):
    size = factor_ref.shape[2]
    half = size // 2
    cols = injection_ref.shape[3]
    tile = size // mask_ref.shape[2]
    position = lax.axis_index("slab")
    core = lax.axis_index("rhs")
    twin = 1 - core
    levels = slabs.bit_length() - 1

    level = jnp.int32(0)
    stride = jnp.int32(1)
    for k in range(1, levels + 1):
        even = jnp.where(position % (1 << k) == 0, 1, 0)
        level = level + even
        stride = stride + even * (1 << (k - 1))
    is_root = position == 0
    not_root = position > 0
    has_right = jnp.logical_and(not_root, position + stride < slabs)
    near_is_right = jnp.logical_and(has_right, (position // stride) % 4 == 1)
    near = jnp.where(near_is_right, 1, 0)
    far = 1 - near
    near_target = jnp.where(near_is_right, position + stride, position - stride)
    far_target = jnp.where(near_is_right, position - stride, position + stride)

    def remote(source, target, sent, received, slab_to, core_to):
        return pltpu.make_async_remote_copy(
            src_ref=source,
            dst_ref=target,
            send_sem=sent,
            recv_sem=received,
            device_id=(slab_to, core_to),
            device_id_type=MESH,
        )

    barrier = pltpu.get_barrier_semaphore()

    def greet(slab_to, core_to):
        pl.semaphore_signal(barrier, inc=1, device_id=(slab_to, core_to), device_id_type=MESH)

    greet(position, twin)
    for k in range(levels):
        step = 1 << k
        pl.when(jnp.logical_and(level >= k, position + step < slabs))(
            functools.partial(greet, position + step, core)
        )
        pl.when(jnp.logical_and(level >= k, position >= step))(
            functools.partial(greet, position - step, core)
        )

    lane = lax.broadcasted_iota(jnp.int32, (1, 128), 1)
    masked = []
    for plane in range(2):
        rows = []
        for r in range(size // tile):
            blocks = []
            for k in range(size // 128):
                keep = mask_ref[0, r, k * 128 // tile].astype(F32)
                for t in range(1, 128 // tile):
                    other = mask_ref[0, r, k * 128 // tile + t].astype(F32)
                    keep = jnp.where(lane >= t * tile, other, keep)
                piece = factor_ref[0, plane, r * tile : (r + 1) * tile, k * 128 : (k + 1) * 128]
                blocks.append(piece * keep)
            rows.append(jnp.concatenate(blocks, 1))
        masked.append(jnp.concatenate(rows, 0))
    left = split(jnp.concatenate(masked, 1))
    turned = [masked[0].T, -masked[1].T]
    right = pair_map(
        lambda planes: planes,
        split(
            jnp.concatenate(
                [jnp.concatenate(turned, 1), jnp.concatenate([-turned[1], turned[0]], 1)], 0
            )
        ),
    )
    bond = dot3(left, right)

    def store_halves(store, value):
        for h in range(2):
            for plane in range(2):
                store(h, plane, value[:, plane * size + h * half : plane * size + (h + 1) * half])

    def keep_out(h, plane, value):
        bond_out[h, plane] = value

    store_halves(keep_out, bond)

    row = lax.broadcasted_iota(jnp.int32, (size, half), 0)
    column = lax.broadcasted_iota(jnp.int32, (size, half), 1) + core * half
    own = jnp.where(
        core == 0, potential_ref[:, 0:half], potential_ref[:, half:size]
    )
    ground[core, 0] = jnp.where(row == column, jnp.broadcast_to(own, (size, half)), 0.0)
    ground[core, 1] = jnp.zeros((size, half), F32)
    waves[...] = jnp.concatenate([injection_ref[0, 0], injection_ref[0, 1]], 1)
    flag[...] = jnp.zeros_like(flag)

    @pl.when(jnp.logical_not(has_right))
    def _():
        coupling[1] = jnp.zeros((2, 2, size, half), F32)

    @pl.when(is_root)
    def _():
        coupling[0] = jnp.zeros((2, 2, size, half), F32)

    @pl.when(position == slabs - 1)
    def _():
        ground[core] = ground[core] + bond_out[core]

    @pl.when(jnp.logical_and(level == 0, has_right))
    def _():
        coupling[1] = bond_out[...]

    partners = jnp.int32(1)
    for k in range(levels):
        step = 1 << k
        partners += jnp.where(jnp.logical_and(level >= k, position + step < slabs), 1, 0)
        partners += jnp.where(jnp.logical_and(level >= k, position >= step), 1, 0)
    pl.semaphore_wait(barrier, partners)

    def bond_copy():
        return remote(
            bond_out.at[core],
            coupling.at[0, core],
            send_sem.at[0],
            bond_sem.at[0],
            position + 1,
            core,
        )

    pl.when(level > 0)(lambda: bond_copy().start())

    def terms_arrival(k, side):
        return remote(
            terms_in.at[k, side], terms_in.at[k, side], send_sem.at[1], terms_sem.at[k, side], position, twin
        )

    def add_terms(k, side):
        terms_arrival(k, side).wait_recv()
        ground[core, 0] += terms_in[k, side, 0:size]
        ground[core, 1] += terms_in[k, side, size : 2 * size]
        waves[...] += terms_in[k, side, 2 * size : 3 * size]
        flag[...] = jnp.maximum(flag[...], terms_in[k, side, 3 * size : 3 * size + 8])

    def add_level(k):
        pl.when(not_root)(functools.partial(add_terms, k, 0))
        add_terms(k, 1)

    @pl.loop(0, jnp.maximum(level - 1, 0))
    def _(k):
        add_level(k)

    def join(block, which):
        return remote(block, block, join_send_sem.at[which], join_sem.at[which], position, twin)

    @pl.when(not_root)
    def _():
        remote(
            coupling.at[0, core], coupling.at[0, core], send_sem.at[1], bond_sem.at[0], position, twin
        ).wait_recv()
        join(coupling.at[0, core], 0).start()

    two_sided = jnp.logical_and(level > 0, has_right)

    @pl.when(two_sided)
    def _():
        remote(
            coupling.at[1, core], coupling.at[1, core], send_sem.at[1], bond_sem.at[1], position, twin
        ).wait_recv()
        join(coupling.at[1, core], 1).start()

    pl.when(level > 0)(lambda: add_level(level - 1))
    join(ground.at[core], 2).start()
    pl.when(not_root)(lambda: join(coupling.at[0, twin], 0).wait_recv())
    pl.when(two_sided)(lambda: join(coupling.at[1, twin], 1).wait_recv())
    join(ground.at[twin], 2).wait_recv()

    def whole(block):
        return jnp.concatenate([block[0, 0], block[1, 0], block[0, 1], block[1, 1]], 1)

    def turn(value):
        width = value.shape[1] // 2
        return jnp.concatenate([-value[:, width:], value[:, :width]], 1)

    def expand(value):
        return jnp.concatenate([value, turn(value)], 0)

    matrix = whole(ground) + whole(coupling.at[0]) + whole(coupling.at[1])
    wide_row = lax.broadcasted_iota(jnp.int32, (size, 2 * size), 0)
    wide_column = lax.broadcasted_iota(jnp.int32, (size, 2 * size), 1)
    unit = jnp.where(wide_row == wide_column, 1.0, 0.0).astype(F32)
    mean = jnp.sum(matrix * unit, keepdims=True) / size
    scale = 1.0 / mean
    scaled = matrix * scale
    power = unit - scaled
    inverse = unit + power
    power = power.astype(BF16)
    power = dot(power, expand(power)).astype(BF16)
    for k in range(3):
        both = dot(jnp.concatenate([inverse.astype(BF16), power], 0), expand(power))
        inverse = inverse + both[:size]
        power = both[size:].astype(BF16)
    inverse = inverse + dot(inverse.astype(BF16), expand(power))
    residual = unit - dot3(split(scaled), pair_map(expand, split(inverse)))
    inverse = inverse + dot(inverse.astype(BF16), expand(residual.astype(BF16)))
    squared = jnp.sum(residual * residual, keepdims=True)
    bad = jnp.where(squared < RESIDUAL_LIMIT, 0.0, 1.0)
    flag[...] = jnp.maximum(flag[...], jnp.broadcast_to(bad, (8, 128)))
    solver = split(inverse * scale)

    def turn_waves(value):
        return jnp.concatenate([-value[:, cols:], value[:, :cols]], 1)

    def expand_waves(value):
        return jnp.concatenate([value, turn_waves(value)], 0)

    solved_waves = dot3(solver, pair_map(expand_waves, split(waves[...])))

    def own_half(block):
        return jnp.concatenate([block[core, 0], block[core, 1]], 1)

    near_copy_bond = remote(
        near_bond,
        coupling.at[far, core],
        send_sem.at[2],
        bond_sem.at[far],
        near_target,
        core,
    )
    near_copy = remote(
        near_out,
        terms_in.at[level, far],
        send_sem.at[3],
        terms_sem.at[level, far],
        near_target,
        core,
    )
    far_copy = remote(
        far_out,
        terms_in.at[level, near],
        send_sem.at[4],
        terms_sem.at[level, near],
        far_target,
        core,
    )

    @pl.when(not_root)
    def _():
        def adjoint_pair(block):
            real = jnp.concatenate([block[0, 0], block[1, 0]], 1).T
            imag = jnp.concatenate([block[0, 1], block[1, 1]], 1).T
            return split(jnp.concatenate([real, -imag], 1))

        near_left = adjoint_pair(coupling.at[near])

        @pl.when(has_right)
        def _():
            solved = dot3(solver, pair_map(expand, split(own_half(coupling.at[far]))))
            product = dot3(near_left, pair_map(expand, split(solved)))
            near_bond[0] = product[:, :half]
            near_bond[1] = product[:, half:]
            near_copy_bond.start()

        solved_ground = pair_map(expand, split(dot3(solver, pair_map(expand, split(own_half(ground))))))
        waves_pair = pair_map(expand_waves, split(solved_waves))

        def fill(out, left_pair):
            product = dot3(left_pair, solved_ground)
            out[0:size] = product[:, :half]
            out[size : 2 * size] = product[:, half:]
            out[2 * size : 3 * size] = dot3(left_pair, waves_pair)
            out[3 * size : 3 * size + 8] = flag[...]

        fill(near_out, near_left)
        near_copy.start()

        @pl.when(has_right)
        def _():
            fill(far_out, adjoint_pair(coupling.at[far]))
            far_copy.start()

        for side in range(2):
            spike = split(dot3(solver, pair_map(expand, split(whole(coupling.at[side])))))
            for part in range(2):
                back[part, :, side * 2 * size : (side + 1) * 2 * size] = spike[part]

    def wave_arrival(side):
        return remote(
            wave_in.at[side], wave_in.at[side], send_sem.at[1], wave_sem.at[side], position, twin
        )

    wave_out[0:size] = solved_waves

    @pl.when(not_root)
    def _():
        def add_side(side):
            wave_arrival(side).wait_recv()
            pair = pair_map(expand_waves, split(wave_in[side, 0:size]))
            spike = (
                back[0, :, side * 2 * size : (side + 1) * 2 * size],
                back[1, :, side * 2 * size : (side + 1) * 2 * size],
            )
            wave_out[0:size] += dot3(spike, pair)

        add_side(0)
        flag[...] = jnp.maximum(flag[...], wave_in[0, size : size + 8])
        pl.when(has_right)(functools.partial(add_side, 1))

    wave_out[size : size + 8] = flag[...]

    @pl.loop(0, level)
    def _(down):
        k = level - 1 - down
        step = jnp.int32(1)
        for m in range(1, levels):
            step = step + jnp.where(k >= m, 1 << (m - 1), 0)
        to_right = remote(
            wave_out, wave_in.at[0], wave_send_sem.at[0], wave_sem.at[0], position + step, core
        )
        to_left = remote(
            wave_out, wave_in.at[1], wave_send_sem.at[1], wave_sem.at[1], position - step, core
        )
        to_right.start()
        pl.when(not_root)(lambda: to_left.start())
        to_right.wait_send()
        pl.when(not_root)(lambda: to_left.wait_send())

    out_ref[0, 0] = wave_out[0:size, :cols]
    out_ref[0, 1] = wave_out[0:size, cols:]
    flag_ref[...] = flag[...]

    pl.when(level > 0)(lambda: bond_copy().wait_send())
    pl.when(not_root)(lambda: join(coupling.at[0, core], 0).wait_send())
    pl.when(two_sided)(lambda: join(coupling.at[1, core], 1).wait_send())
    join(ground.at[core], 2).wait_send()
    pl.when(not_root)(lambda: near_copy.wait_send())

    @pl.when(has_right)
    def _():
        near_copy_bond.wait_send()
        far_copy.wait_send()


def tree_path(slabs, bond_factor, tile_mask, potential, injection):
    size = bond_factor.shape[2]
    half = size // 2
    levels = slabs.bit_length() - 1
    vmem = pl.BlockSpec(memory_space=pltpu.VMEM)
    rows = 3 * size + 8
    return pl.pallas_call(
        functools.partial(tree_kernel, slabs),
        out_shape=(
            jax.ShapeDtypeStruct(injection.shape, F32),
            jax.ShapeDtypeStruct((8, 128), F32),
        ),
        in_specs=[vmem, pl.BlockSpec(memory_space=pltpu.SMEM), vmem, vmem],
        out_specs=(vmem, vmem),
        scratch_shapes=[
            pltpu.VMEM((2, 2, size, half), F32),
            pltpu.VMEM((2, 2, 2, size, half), F32),
            pltpu.VMEM((size, 128), F32),
            pltpu.VMEM((8, 128), F32),
            pltpu.VMEM((2, 2, size, half), F32),
            pltpu.VMEM((2, size, half), F32),
            pltpu.VMEM((rows, 128), F32),
            pltpu.VMEM((rows, 128), F32),
            pltpu.VMEM((levels, 2, rows, 128), F32),
            pltpu.VMEM((2, size + 8, 128), F32),
            pltpu.VMEM((size + 8, 128), F32),
            pltpu.VMEM((2, size, 4 * size), BF16),
            pltpu.SemaphoreType.DMA((5,)),
            pltpu.SemaphoreType.DMA((2,)),
            pltpu.SemaphoreType.DMA((levels, 2)),
            pltpu.SemaphoreType.DMA((2,)),
            pltpu.SemaphoreType.DMA((2,)),
            pltpu.SemaphoreType.DMA((3,)),
            pltpu.SemaphoreType.DMA((3,)),
        ],
        compiler_params=pltpu.CompilerParams(
            collective_id=0, has_side_effects=True, vmem_limit_bytes=48 << 20
        ),
        name="tree_reduction",
    )(bond_factor, tile_mask, potential, injection)


def per_device(slabs, bond_factor, tile_mask, potential, injection):
    amplitude, flag = tree_path(slabs, bond_factor, tile_mask, potential, injection)
    return lax.cond(
        flag[0, 0] == 0.0,
        lambda *operands: amplitude,
        direct_path,
        bond_factor,
        tile_mask,
        potential,
        injection,
    )


def solution(mesh):
    in_specs = (
        P("slab", None, None, None),
        P("slab", None, None),
        P("slab", None),
        P("slab", None, None, "rhs"),
    )
    out_specs = P("slab", None, None, "rhs")
    return jax.shard_map(
        functools.partial(per_device, mesh.shape["slab"]),
        mesh=mesh,
        in_specs=in_specs,
        out_specs=out_specs,
        check_vma=False,
    )
```

```python
import functools

import jax
import jax.numpy as jnp
from jax import lax
from jax.experimental import pallas as pl
from jax.experimental.pallas import tpu as pltpu
from jax.sharding import PartitionSpec as P

PRECISE = lax.Precision.HIGHEST
MESH = pl.DeviceIdType.MESH
F32 = jnp.float32
BF16 = jnp.bfloat16
RESIDUAL_LIMIT = 4.0e-4


def passed_along(array, axis, by):
    length = lax.axis_size(axis)
    pairs = [(i, i + by) for i in range(length) if 0 <= i + by < length]
    return lax.ppermute(array, axis, pairs)


def matmul_exact(operand, other):
    return jnp.dot(operand, other, precision=PRECISE)


def transposed_product(operand, other):
    return lax.dot_general(operand, other, (((0,), (0,)), ((), ())), precision=PRECISE)


def complex_product(operand, other):
    real_part = matmul_exact(operand[0], other[0]) - matmul_exact(operand[1], other[1])
    imag_part = matmul_exact(operand[0], other[1]) + matmul_exact(operand[1], other[0])
    return jnp.stack([real_part, imag_part])


def adjoint_product(operand, other):
    real_part = transposed_product(operand[0], other[0]) + transposed_product(operand[1], other[1])
    imag_part = transposed_product(operand[0], other[1]) - transposed_product(operand[1], other[0])
    return jnp.stack([real_part, imag_part])


def adjoint(operand):
    return jnp.stack([operand[0].T, -operand[1].T])


def real_form(matrix):
    return jnp.block([[matrix[0], -matrix[1]], [matrix[1], matrix[0]]])


def solve_stacked(factor_low, stacked):
    forward_part = lax.linalg.triangular_solve(factor_low, stacked, left_side=True, lower=True)
    return lax.linalg.triangular_solve(
        factor_low, forward_part, left_side=True, lower=True, transpose_a=True
    )


def direct_path(bond_factor, tile_mask, potential, injection):
    orbitals = bond_factor.shape[2]
    tile_size = orbitals // tile_mask.shape[2]
    slab_total = lax.axis_size("slab")
    position = lax.axis_index("slab")
    core_total = lax.axis_size("rhs")
    core_index = lax.axis_index("rhs")
    half_cols = orbitals // core_total
    pattern = jnp.repeat(jnp.repeat(tile_mask[0], tile_size, 0), tile_size, 1).astype(
        bond_factor.dtype
    )
    factor = bond_factor[0] * pattern[None]
    bond_matrix = complex_product(factor, adjoint(factor))
    previous = passed_along(bond_matrix, "slab", 1)
    onsite = jnp.stack([jnp.diag(potential[0]), jnp.zeros((orbitals, orbitals), potential.dtype)])
    matrix = onsite + bond_matrix + previous
    coupling_up = jnp.where(position == slab_total - 1, jnp.zeros_like(bond_matrix), -bond_matrix)
    coupling_down = -previous
    sources = injection[0]

    def apply_inverse(block, right_side):
        factor_low = jnp.linalg.cholesky(real_form(block))
        stacked = jnp.concatenate([right_side[0], right_side[1]], 0)
        solved = solve_stacked(factor_low, stacked)
        return jnp.stack([solved[:orbitals], solved[orbitals:]])

    def own_columns(block):
        return lax.dynamic_slice_in_dim(block, core_index * half_cols, half_cols, 2)

    levels = slab_total.bit_length() - 1
    for rank_bit in range(levels):
        stride = 1 << rank_bit
        spikes = apply_inverse(
            matrix,
            jnp.concatenate([own_columns(coupling_up), own_columns(coupling_down), sources], 2),
        )
        spike_up = spikes[:, :, :half_cols]
        spike_down = spikes[:, :, half_cols : 2 * half_cols]
        spike_waves = spikes[:, :, 2 * half_cols :]
        toward_upper = adjoint_product(
            coupling_down, jnp.concatenate([spike_down, spike_up, spike_waves], 2)
        )
        from_upper = passed_along(toward_upper, "slab", -stride)
        cross_part = toward_upper[:, :, half_cols : 2 * half_cols]
        toward_lower = adjoint_product(coupling_up, jnp.concatenate([spike_up, spike_waves], 2))
        outgoing = jnp.concatenate(
            [toward_lower[:, :, :half_cols], cross_part, toward_lower[:, :, half_cols:]], 2
        )
        from_lower = passed_along(outgoing, "slab", stride)
        diag_change = from_upper[:, :, :half_cols] + from_lower[:, :, :half_cols]
        new_up = -from_upper[:, :, half_cols : 2 * half_cols]
        coupling_new = from_lower[:, :, half_cols : 2 * half_cols]
        sources = sources - from_upper[:, :, 2 * half_cols :] - from_lower[:, :, 2 * half_cols :]
        gathered = (
            lax.all_gather(diag_change, "rhs", axis=2, tiled=True),
            lax.all_gather(new_up, "rhs", axis=2, tiled=True),
            lax.all_gather(coupling_new, "rhs", axis=2, tiled=True),
        )
        matrix = matrix - gathered[0]
        coupling_up = gathered[1]
        coupling_down = -adjoint(gathered[2])
    amplitude = apply_inverse(matrix, sources)
    return amplitude[None]


def split(value):
    high = value.astype(BF16)
    low = (value - high.astype(F32)).astype(BF16)
    return high, low


def dot(left, right):
    return jnp.dot(left, right, preferred_element_type=F32)


def dot3(left, right):
    high = dot(left[0], right[0])
    return high + (dot(left[0], right[1]) + dot(left[1], right[0]))


def pair_map(function, pair):
    return function(pair[0]), function(pair[1])


def tree_kernel(
    slabs,
    factor_ref,
    mask_ref,
    potential_ref,
    injection_ref,
    out_ref,
    flag_ref,
    ground,
    links,
    matrix,
    spare,
    waves,
    flag,
    bond_out,
    bond_in,
    corner_out,
    corner_in,
    ground_out,
    ground_in,
    waves_out,
    waves_in,
    link_out,
    link_in,
    far_out,
    terms_in,
    wave_in,
    wave_out,
    back,
    send_sem,
    bond_sem,
    corner_sem,
    ground_sem,
    waves_sem,
    link_sem,
    terms_sem,
    wave_sem,
    wave_send_sem,
    join_send_sem,
    join_sem,
):
    size = factor_ref.shape[2]
    half = size // 2
    cols = injection_ref.shape[3]
    tile = size // mask_ref.shape[2]
    position = lax.axis_index("slab")
    core = lax.axis_index("rhs")
    twin = 1 - core
    levels = slabs.bit_length() - 1

    level = jnp.int32(0)
    stride = jnp.int32(1)
    for k in range(1, levels + 1):
        even = jnp.where(position % (1 << k) == 0, 1, 0)
        level = level + even
        stride = stride + even * (1 << (k - 1))
    not_root = position > 0
    inner = level > 0
    inner_left = jnp.logical_and(inner, not_root)
    deep = level > 1
    deep_left = jnp.logical_and(deep, not_root)
    shallow = position % 4 != 0
    has_right = jnp.logical_and(not_root, position + stride < slabs)
    near_is_right = jnp.logical_and(has_right, (position // stride) % 4 == 1)
    near = jnp.where(near_is_right, 1, 0)
    far = 1 - near
    near_target = jnp.where(near_is_right, position + stride, position - stride)
    far_target = jnp.where(near_is_right, position - stride, position + stride)
    near_is_root = near_target == 0
    sends_ground = jnp.logical_and(not_root, jnp.logical_not(near_is_root))
    sends_link = jnp.logical_and(
        has_right, jnp.logical_or((far_target // stride) % 8 == 4, jnp.logical_and(far_target == 0, stride * 4 == slabs))
    )
    sends_bond = (position + 1) % 4 != 0

    def remote(source, target, sent, received, slab_to, core_to):
        return pltpu.make_async_remote_copy(
            src_ref=source,
            dst_ref=target,
            send_sem=sent,
            recv_sem=received,
            device_id=(slab_to, core_to),
            device_id_type=MESH,
        )

    def arrival(block, received):
        return remote(block, block, send_sem.at[1], received, position, twin)

    def join(block, which):
        return remote(block, block, join_send_sem.at[which], join_sem.at[which], position, twin)

    row = lax.broadcasted_iota(jnp.int32, (size, half), 0)
    lane_half = lax.broadcasted_iota(jnp.int32, (size, half), 1)
    column = lane_half + core * half
    square_row = lax.broadcasted_iota(jnp.int32, (size, size), 0)
    square_column = lax.broadcasted_iota(jnp.int32, (size, size), 1)
    own_real = pl.ds(pl.multiple_of(core * half, half), half)
    own_imag = pl.ds(pl.multiple_of(core * half + size, half), half)

    for h in range(2):
        energies = jnp.broadcast_to(potential_ref[:, h * half : (h + 1) * half], (size, half))
        ground[h, 0] = jnp.where(row == lane_half + h * half, energies, 0.0)
        ground[h, 1] = jnp.zeros((size, half), F32)

    barrier = pltpu.get_barrier_semaphore()

    def greet(slab_to, core_to):
        pl.semaphore_signal(barrier, inc=1, device_id=(slab_to, core_to), device_id_type=MESH)

    greet(position, twin)
    for k in range(levels):
        step = 1 << k
        pl.when(jnp.logical_and(level >= k, position + step < slabs))(
            functools.partial(greet, position + step, core)
        )
        pl.when(jnp.logical_and(level >= k, position >= step))(
            functools.partial(greet, position - step, core)
        )

    def turn(value):
        width = value.shape[1] // 2
        return jnp.concatenate([-value[:, width:], value[:, :width]], 1)

    def expand(value):
        return jnp.concatenate([value, turn(value)], 0)

    def adjoint_of(value):
        return jnp.concatenate([value[:, :size].T, -value[:, size:].T], 1)

    def unpack(square):
        turned = square.T
        real = jnp.where(square_row >= square_column, square, turned)
        below = jnp.where(square_row > square_column, -turned, 0.0)
        imag = jnp.where(square_row < square_column, square, below)
        return jnp.concatenate([real, imag], 1)

    def both_halves(block):
        return jnp.concatenate([block[0], block[1]], 1)

    def whole(block):
        return jnp.concatenate([block[0, 0], block[1, 0], block[0, 1], block[1, 1]], 1)

    lane = lax.broadcasted_iota(jnp.int32, (1, 128), 1)
    masked = []
    for plane in range(2):
        rows = []
        for r in range(size // tile):
            blocks = []
            for k in range(size // 128):
                keep = mask_ref[0, r, k * 128 // tile].astype(F32)
                for t in range(1, 128 // tile):
                    other = mask_ref[0, r, k * 128 // tile + t].astype(F32)
                    keep = jnp.where(lane >= t * tile, other, keep)
                piece = factor_ref[0, plane, r * tile : (r + 1) * tile, k * 128 : (k + 1) * 128]
                blocks.append(piece * keep)
            rows.append(jnp.concatenate(blocks, 1))
        masked.append(jnp.concatenate(rows, 0))
    factor = jnp.concatenate(masked, 1)
    bond = dot3(split(factor), pair_map(expand, split(adjoint_of(factor))))
    packed = jnp.where(square_row >= square_column, bond[:, :size], bond[:, size:])
    bond_out[0] = packed[:, :half]
    bond_out[1] = packed[:, half:]

    waves[...] = jnp.concatenate([injection_ref[0, 0], injection_ref[0, 1]], 1)
    flag[...] = jnp.zeros_like(flag)

    partners = jnp.int32(1)
    for k in range(levels):
        step = 1 << k
        partners += jnp.where(jnp.logical_and(level >= k, position + step < slabs), 1, 0)
        partners += jnp.where(jnp.logical_and(level >= k, position >= step), 1, 0)
    pl.semaphore_wait(barrier, partners)

    def bond_copy():
        return remote(
            bond_out.at[core], bond_in.at[core], send_sem.at[0], bond_sem.at[0], position + 1, core
        )

    pl.when(sends_bond)(lambda: bond_copy().start())

    @pl.when(shallow)
    def _():
        arrival(bond_in.at[core], bond_sem.at[0]).wait_recv()
        join(bond_in.at[core], 0).start()
        own_bond = unpack(both_halves(bond_out))

        @pl.when(position < slabs - 1)
        def _():
            links[1] = own_bond

        @pl.when(position == slabs - 1)
        def _():
            for h in range(2):
                for plane in range(2):
                    first = plane * size + h * half
                    ground[h, plane] += own_bond[:, first : first + half]
            links[1] = jnp.zeros((size, 2 * size), F32)

        join(bond_in.at[twin], 0).wait_recv()
        links[0] = unpack(both_halves(bond_in))

    def add_terms(k, side):
        arrival(terms_in.at[k, side], terms_sem.at[k, side]).wait_recv()
        ground[core, 0] += terms_in[k, side, 0:size]
        ground[core, 1] += terms_in[k, side, size : 2 * size]
        waves[...] += terms_in[k, side, 2 * size : 3 * size]
        flag[...] = jnp.maximum(flag[...], terms_in[k, side, 3 * size : 3 * size + 8])

    @pl.loop(0, jnp.maximum(level - 1, 0))
    def _(k):
        pl.when(not_root)(functools.partial(add_terms, k, 0))
        add_terms(k, 1)

    pl.when(inner)(lambda: join(ground.at[core], 5).start())

    def link_arrival(side):
        arrival(link_in.at[side, core], link_sem.at[side]).wait_recv()
        join(link_in.at[side, core], 6 + side).start()

    def link_whole(side):
        join(link_in.at[side, twin], 6 + side).wait_recv()
        links[side] = adjoint_of(whole(link_in.at[side]))

    pl.when(deep_left)(functools.partial(link_arrival, 0))
    pl.when(deep)(functools.partial(link_arrival, 1))
    pl.when(deep_left)(functools.partial(link_whole, 0))
    pl.when(deep)(functools.partial(link_whole, 1))

    @pl.when(jnp.logical_not(not_root))
    def _():
        links[0] = jnp.zeros((size, 2 * size), F32)

    pl.when(inner)(lambda: join(ground.at[twin], 5).wait_recv())
    matrix[...] = whole(ground) + links[0] + links[1]

    def corner_arrival(side):
        arrival(corner_in.at[side, core], corner_sem.at[side]).wait_recv()
        join(corner_in.at[side, core], 1 + side).start()

    def corner_whole(side):
        join(corner_in.at[side, twin], 1 + side).wait_recv()
        term = unpack(both_halves(corner_in.at[side]))
        matrix[...] -= term
        links[side] -= term

    pl.when(inner_left)(functools.partial(corner_arrival, 0))
    pl.when(inner)(functools.partial(corner_arrival, 1))
    pl.when(inner_left)(functools.partial(corner_whole, 0))
    pl.when(inner)(functools.partial(corner_whole, 1))

    wide_row = lax.broadcasted_iota(jnp.int32, (size, 2 * size), 0)
    wide_column = lax.broadcasted_iota(jnp.int32, (size, 2 * size), 1)
    unit = jnp.where(wide_row == wide_column, 1.0, 0.0).astype(F32)
    mean = jnp.sum(matrix[...] * unit, keepdims=True) / size
    scale = 1.0 / mean
    scaled = matrix[...] * scale
    power = unit - scaled
    inverse = unit + power
    power = power.astype(BF16)
    power = dot(power, expand(power)).astype(BF16)
    for k in range(3):
        both = dot(jnp.concatenate([inverse.astype(BF16), power], 0), expand(power))
        inverse = inverse + both[:size]
        power = both[size:].astype(BF16)
    inverse = inverse + dot(inverse.astype(BF16), expand(power))
    inverse_pair = split(inverse)
    residual = unit - dot3(split(scaled), pair_map(expand, inverse_pair))
    inverse = inverse + dot3(inverse_pair, pair_map(expand, split(residual)))
    squared = jnp.sum(residual * residual, keepdims=True)
    bad = jnp.where(squared < RESIDUAL_LIMIT, 0.0, 1.0)
    flag[...] = jnp.maximum(flag[...], jnp.broadcast_to(bad, (8, 128)))
    solver = split(inverse * scale)

    def ground_arrival(side):
        arrival(ground_in.at[side, core], ground_sem.at[side]).wait_recv()
        join(ground_in.at[side, core], 3 + side).start()

    def ground_whole(side):
        join(ground_in.at[side, twin], 3 + side).wait_recv()
        links[side] -= whole(ground_in.at[side])
        ground[core] += ground_in[side, core]

    pl.when(inner_left)(functools.partial(ground_arrival, 0))
    pl.when(inner_left)(functools.partial(ground_arrival, 1))
    pl.when(inner)(lambda: join(ground.at[core], 5).wait_send())
    pl.when(inner_left)(functools.partial(ground_whole, 0))
    pl.when(inner_left)(functools.partial(ground_whole, 1))

    @pl.when(jnp.logical_not(has_right))
    def _():
        links[1] = jnp.zeros((size, 2 * size), F32)

    corner_copy = remote(
        corner_out.at[core],
        corner_in.at[far, core],
        send_sem.at[2],
        corner_sem.at[far],
        near_target,
        core,
    )
    ground_copy = remote(
        ground_out, ground_in.at[far, core], send_sem.at[3], ground_sem.at[far], near_target, core
    )
    waves_copy = remote(
        waves_out, waves_in.at[far], send_sem.at[4], waves_sem.at[far], near_target, core
    )
    far_copy = remote(
        far_out, terms_in.at[level, near], send_sem.at[5], terms_sem.at[level, near], far_target, core
    )
    link_copy = remote(
        link_out, link_in.at[near, core], send_sem.at[6], link_sem.at[near], far_target, core
    )

    def own_half(ref):
        return jnp.concatenate([ref[:, own_real], ref[:, own_imag]], 1)

    def add_waves(side):
        arrival(waves_in.at[side], waves_sem.at[side]).wait_recv()
        waves[...] += waves_in[side, 0:size]
        flag[...] = jnp.maximum(flag[...], waves_in[side, size : size + 8])

    def solve_waves():
        pl.when(inner_left)(functools.partial(add_waves, 0))
        pl.when(inner)(functools.partial(add_waves, 1))
        solved = dot3(solver, pair_map(expand, split(waves[...])))
        wave_out[0:size] = solved
        return pair_map(expand, split(solved))

    @pl.when(jnp.logical_not(not_root))
    def _():
        solve_waves()

    @pl.when(not_root)
    def _():
        near_adjoint = adjoint_of(links[near])
        near_left = split(near_adjoint)
        solved = dot3(solver, pair_map(expand, split(own_half(links.at[near]))))
        solved_near = pair_map(expand, split(solved))
        product = dot3(near_left, solved_near)
        corner_out[core] = jnp.where(row >= column, product[:, :half], product[:, half:])
        corner_copy.start()

        own_ground = jnp.concatenate([ground[core, 0], ground[core, 1]], 1)
        solved = dot3(solver, pair_map(expand, split(own_ground)))
        solved_ground = pair_map(expand, split(solved))

        product = dot3(near_left, solved_ground)
        ground_out[0] = product[:, :half]
        ground_out[1] = product[:, half:]
        pl.when(sends_ground)(lambda: ground_copy.start())

        solved_waves = solve_waves()
        waves_out[0:size] = dot3(near_left, solved_waves)
        waves_out[size : size + 8] = flag[...]
        waves_copy.start()

        @pl.when(has_right)
        def _():
            far_left = split(adjoint_of(links[far]))
            product = dot3(far_left, solved_ground)
            far_out[0:size] = product[:, :half]
            far_out[size : 2 * size] = product[:, half:]
            far_out[2 * size : 3 * size] = dot3(far_left, solved_waves)
            far_out[3 * size : 3 * size + 8] = flag[...]
            far_copy.start()

        @pl.when(sends_link)
        def _():
            join(corner_out.at[core], 8).start()
            join(corner_out.at[twin], 8).wait_recv()
            spare[...] = near_adjoint - unpack(both_halves(corner_out))
            link_out[0] = spare[:, own_real] - ground_out[0]
            link_out[1] = spare[:, own_imag] - ground_out[1]
            link_copy.start()

        for side in range(2):
            spike = split(dot3(solver, pair_map(expand, split(links[side]))))
            for part in range(2):
                back[part, :, side * 2 * size : (side + 1) * 2 * size] = spike[part]

    def add_side(side):
        arrival(wave_in.at[side], wave_sem.at[side]).wait_recv()
        pair = pair_map(expand, split(wave_in[side, 0:size]))
        spike = (
            back[0, :, side * 2 * size : (side + 1) * 2 * size],
            back[1, :, side * 2 * size : (side + 1) * 2 * size],
        )
        wave_out[0:size] += dot3(spike, pair)

    @pl.when(not_root)
    def _():
        add_side(0)
        flag[...] = jnp.maximum(flag[...], wave_in[0, size : size + 8])
        pl.when(has_right)(functools.partial(add_side, 1))

    wave_out[size : size + 8] = flag[...]

    @pl.loop(0, level)
    def _(down):
        k = level - 1 - down
        step = jnp.int32(1)
        for m in range(1, levels):
            step = step + jnp.where(k >= m, 1 << (m - 1), 0)
        to_right = remote(
            wave_out, wave_in.at[0], wave_send_sem.at[0], wave_sem.at[0], position + step, core
        )
        to_left = remote(
            wave_out, wave_in.at[1], wave_send_sem.at[1], wave_sem.at[1], position - step, core
        )
        to_right.start()
        pl.when(not_root)(lambda: to_left.start())
        to_right.wait_send()
        pl.when(not_root)(lambda: to_left.wait_send())

    out_ref[0, 0] = wave_out[0:size, :cols]
    out_ref[0, 1] = wave_out[0:size, cols:]
    flag_ref[...] = flag[...]

    pl.when(sends_bond)(lambda: bond_copy().wait_send())
    pl.when(shallow)(lambda: join(bond_in.at[core], 0).wait_send())
    for side in range(2):
        pl.when(deep_left if side == 0 else deep)(
            lambda: join(link_in.at[side, core], 6 + side).wait_send()
        )
        pl.when(inner_left if side == 0 else inner)(
            lambda: join(corner_in.at[side, core], 1 + side).wait_send()
        )
        pl.when(inner_left)(lambda: join(ground_in.at[side, core], 3 + side).wait_send())

    @pl.when(not_root)
    def _():
        corner_copy.wait_send()
        pl.when(sends_ground)(lambda: ground_copy.wait_send())
        waves_copy.wait_send()
        pl.when(has_right)(lambda: far_copy.wait_send())

    @pl.when(sends_link)
    def _():
        join(corner_out.at[core], 8).wait_send()
        link_copy.wait_send()


def tree_path(slabs, bond_factor, tile_mask, potential, injection):
    size = bond_factor.shape[2]
    half = size // 2
    levels = slabs.bit_length() - 1
    vmem = pl.BlockSpec(memory_space=pltpu.VMEM)
    rows = 3 * size + 8
    dma = pltpu.SemaphoreType.DMA
    return pl.pallas_call(
        functools.partial(tree_kernel, slabs),
        out_shape=(
            jax.ShapeDtypeStruct(injection.shape, F32),
            jax.ShapeDtypeStruct((8, 128), F32),
        ),
        in_specs=[vmem, pl.BlockSpec(memory_space=pltpu.SMEM), vmem, vmem],
        out_specs=(vmem, vmem),
        scratch_shapes=[
            pltpu.VMEM((2, 2, size, half), F32),
            pltpu.VMEM((2, size, 2 * size), F32),
            pltpu.VMEM((size, 2 * size), F32),
            pltpu.VMEM((size, 2 * size), F32),
            pltpu.VMEM((size, 128), F32),
            pltpu.VMEM((8, 128), F32),
            pltpu.VMEM((2, size, half), F32),
            pltpu.VMEM((2, size, half), F32),
            pltpu.VMEM((2, size, half), F32),
            pltpu.VMEM((2, 2, size, half), F32),
            pltpu.VMEM((2, size, half), F32),
            pltpu.VMEM((2, 2, 2, size, half), F32),
            pltpu.VMEM((size + 8, 128), F32),
            pltpu.VMEM((2, size + 8, 128), F32),
            pltpu.VMEM((2, size, half), F32),
            pltpu.VMEM((2, 2, 2, size, half), F32),
            pltpu.VMEM((rows, 128), F32),
            pltpu.VMEM((levels, 2, rows, 128), F32),
            pltpu.VMEM((2, size + 8, 128), F32),
            pltpu.VMEM((size + 8, 128), F32),
            pltpu.VMEM((2, size, 4 * size), BF16),
            dma((7,)),
            dma((1,)),
            dma((2,)),
            dma((2,)),
            dma((2,)),
            dma((2,)),
            dma((levels, 2)),
            dma((2,)),
            dma((2,)),
            dma((9,)),
            dma((9,)),
        ],
        compiler_params=pltpu.CompilerParams(
            collective_id=0, has_side_effects=True, vmem_limit_bytes=52 << 20
        ),
        name="tree_reduction",
    )(bond_factor, tile_mask, potential, injection)


def per_device(slabs, bond_factor, tile_mask, potential, injection):
    amplitude, flag = tree_path(slabs, bond_factor, tile_mask, potential, injection)
    return lax.cond(
        flag[0, 0] == 0.0,
        lambda *operands: amplitude,
        direct_path,
        bond_factor,
        tile_mask,
        potential,
        injection,
    )


def solution(mesh):
    in_specs = (
        P("slab", None, None, None),
        P("slab", None, None),
        P("slab", None),
        P("slab", None, None, "rhs"),
    )
    out_specs = P("slab", None, None, "rhs")
    return jax.shard_map(
        functools.partial(per_device, mesh.shape["slab"]),
        mesh=mesh,
        in_specs=in_specs,
        out_specs=out_specs,
        check_vma=False,
    )
```

```python
import functools

import jax
import jax.numpy as jnp
from jax import lax
from jax.experimental import pallas as pl
from jax.experimental.pallas import tpu as pltpu
from jax.sharding import PartitionSpec as P

PRECISE = lax.Precision.HIGHEST
MESH = pl.DeviceIdType.MESH
F32 = jnp.float32
BF16 = jnp.bfloat16
RESIDUAL_LIMIT = 4.0e-4


def passed_along(array, axis, by):
    length = lax.axis_size(axis)
    pairs = [(i, i + by) for i in range(length) if 0 <= i + by < length]
    return lax.ppermute(array, axis, pairs)


def matmul_exact(operand, other):
    return jnp.dot(operand, other, precision=PRECISE)


def transposed_product(operand, other):
    return lax.dot_general(operand, other, (((0,), (0,)), ((), ())), precision=PRECISE)


def complex_product(operand, other):
    real_part = matmul_exact(operand[0], other[0]) - matmul_exact(operand[1], other[1])
    imag_part = matmul_exact(operand[0], other[1]) + matmul_exact(operand[1], other[0])
    return jnp.stack([real_part, imag_part])


def adjoint_product(operand, other):
    real_part = transposed_product(operand[0], other[0]) + transposed_product(operand[1], other[1])
    imag_part = transposed_product(operand[0], other[1]) - transposed_product(operand[1], other[0])
    return jnp.stack([real_part, imag_part])


def adjoint(operand):
    return jnp.stack([operand[0].T, -operand[1].T])


def real_form(matrix):
    return jnp.block([[matrix[0], -matrix[1]], [matrix[1], matrix[0]]])


def solve_stacked(factor_low, stacked):
    forward_part = lax.linalg.triangular_solve(factor_low, stacked, left_side=True, lower=True)
    return lax.linalg.triangular_solve(
        factor_low, forward_part, left_side=True, lower=True, transpose_a=True
    )


def direct_path(bond_factor, tile_mask, potential, injection):
    orbitals = bond_factor.shape[2]
    tile_size = orbitals // tile_mask.shape[2]
    slab_total = lax.axis_size("slab")
    position = lax.axis_index("slab")
    core_total = lax.axis_size("rhs")
    core_index = lax.axis_index("rhs")
    half_cols = orbitals // core_total
    pattern = jnp.repeat(jnp.repeat(tile_mask[0], tile_size, 0), tile_size, 1).astype(
        bond_factor.dtype
    )
    factor = bond_factor[0] * pattern[None]
    bond_matrix = complex_product(factor, adjoint(factor))
    previous = passed_along(bond_matrix, "slab", 1)
    onsite = jnp.stack([jnp.diag(potential[0]), jnp.zeros((orbitals, orbitals), potential.dtype)])
    matrix = onsite + bond_matrix + previous
    coupling_up = jnp.where(position == slab_total - 1, jnp.zeros_like(bond_matrix), -bond_matrix)
    coupling_down = -previous
    sources = injection[0]

    def apply_inverse(block, right_side):
        factor_low = jnp.linalg.cholesky(real_form(block))
        stacked = jnp.concatenate([right_side[0], right_side[1]], 0)
        solved = solve_stacked(factor_low, stacked)
        return jnp.stack([solved[:orbitals], solved[orbitals:]])

    def own_columns(block):
        return lax.dynamic_slice_in_dim(block, core_index * half_cols, half_cols, 2)

    levels = slab_total.bit_length() - 1
    for rank_bit in range(levels):
        stride = 1 << rank_bit
        spikes = apply_inverse(
            matrix,
            jnp.concatenate([own_columns(coupling_up), own_columns(coupling_down), sources], 2),
        )
        spike_up = spikes[:, :, :half_cols]
        spike_down = spikes[:, :, half_cols : 2 * half_cols]
        spike_waves = spikes[:, :, 2 * half_cols :]
        toward_upper = adjoint_product(
            coupling_down, jnp.concatenate([spike_down, spike_up, spike_waves], 2)
        )
        from_upper = passed_along(toward_upper, "slab", -stride)
        cross_part = toward_upper[:, :, half_cols : 2 * half_cols]
        toward_lower = adjoint_product(coupling_up, jnp.concatenate([spike_up, spike_waves], 2))
        outgoing = jnp.concatenate(
            [toward_lower[:, :, :half_cols], cross_part, toward_lower[:, :, half_cols:]], 2
        )
        from_lower = passed_along(outgoing, "slab", stride)
        diag_change = from_upper[:, :, :half_cols] + from_lower[:, :, :half_cols]
        new_up = -from_upper[:, :, half_cols : 2 * half_cols]
        coupling_new = from_lower[:, :, half_cols : 2 * half_cols]
        sources = sources - from_upper[:, :, 2 * half_cols :] - from_lower[:, :, 2 * half_cols :]
        gathered = (
            lax.all_gather(diag_change, "rhs", axis=2, tiled=True),
            lax.all_gather(new_up, "rhs", axis=2, tiled=True),
            lax.all_gather(coupling_new, "rhs", axis=2, tiled=True),
        )
        matrix = matrix - gathered[0]
        coupling_up = gathered[1]
        coupling_down = -adjoint(gathered[2])
    amplitude = apply_inverse(matrix, sources)
    return amplitude[None]


def split(value):
    high = value.astype(BF16)
    low = (value - high.astype(F32)).astype(BF16)
    return high, low


def dot(left, right):
    return jnp.dot(left, right, preferred_element_type=F32)


def dot3(left, right):
    high = dot(left[0], right[0])
    return high + (dot(left[0], right[1]) + dot(left[1], right[0]))


def pair_map(function, pair):
    return function(pair[0]), function(pair[1])


def tree_kernel(
    slabs,
    factor_ref,
    mask_ref,
    potential_ref,
    injection_ref,
    out_ref,
    flag_ref,
    ground,
    links,
    matrix,
    spare,
    waves,
    flag,
    bond_out,
    bond_in,
    corner_out,
    corner_in,
    ground_out,
    ground_in,
    waves_out,
    far_waves_out,
    waves_in,
    link_out,
    link_in,
    far_out,
    terms_in,
    wave_in,
    wave_out,
    back,
    send_sem,
    bond_sem,
    corner_sem,
    ground_sem,
    waves_sem,
    link_sem,
    terms_sem,
    wave_sem,
    wave_send_sem,
    join_send_sem,
    join_sem,
):
    size = factor_ref.shape[2]
    half = size // 2
    cols = injection_ref.shape[2]
    tile = size // mask_ref.shape[2]
    position = lax.axis_index("slab")
    core = lax.axis_index("rhs")
    twin = 1 - core
    levels = slabs.bit_length() - 1

    level = jnp.int32(0)
    stride = jnp.int32(1)
    for k in range(1, levels + 1):
        even = jnp.where(position % (1 << k) == 0, 1, 0)
        level = level + even
        stride = stride + even * (1 << (k - 1))
    not_root = position > 0
    inner = level > 0
    inner_left = jnp.logical_and(inner, not_root)
    deep = level > 1
    deep_left = jnp.logical_and(deep, not_root)
    shallow = position % 4 != 0
    has_right = jnp.logical_and(not_root, position + stride < slabs)
    near_is_right = jnp.logical_and(has_right, (position // stride) % 4 == 1)
    near = jnp.where(near_is_right, 1, 0)
    far = 1 - near
    near_target = jnp.where(near_is_right, position + stride, position - stride)
    far_target = jnp.where(near_is_right, position - stride, position + stride)
    near_is_root = near_target == 0
    sends_ground = jnp.logical_and(not_root, jnp.logical_not(near_is_root))
    sends_link = jnp.logical_and(
        has_right, jnp.logical_or((far_target // stride) % 8 == 4, jnp.logical_and(far_target == 0, stride * 4 == slabs))
    )
    sends_bond = (position + 1) % 4 != 0

    def remote(source, target, sent, received, slab_to, core_to):
        return pltpu.make_async_remote_copy(
            src_ref=source,
            dst_ref=target,
            send_sem=sent,
            recv_sem=received,
            device_id=(slab_to, core_to),
            device_id_type=MESH,
        )

    def arrival(block, received):
        return remote(block, block, send_sem.at[1], received, position, twin)

    def join(block, which):
        return remote(block, block, join_send_sem.at[which], join_sem.at[which], position, twin)

    row = lax.broadcasted_iota(jnp.int32, (size, half), 0)
    lane_half = lax.broadcasted_iota(jnp.int32, (size, half), 1)
    column = lane_half + core * half
    square_row = lax.broadcasted_iota(jnp.int32, (size, size), 0)
    square_column = lax.broadcasted_iota(jnp.int32, (size, size), 1)
    own_real = pl.ds(pl.multiple_of(core * half, half), half)
    own_imag = pl.ds(pl.multiple_of(core * half + size, half), half)

    for h in range(2):
        energies = jnp.broadcast_to(potential_ref[:, h * half : (h + 1) * half], (size, half))
        ground[h, 0] = jnp.where(row == lane_half + h * half, energies, 0.0)
        ground[h, 1] = jnp.zeros((size, half), F32)

    barrier = pltpu.get_barrier_semaphore()

    def greet(slab_to, core_to):
        pl.semaphore_signal(barrier, inc=1, device_id=(slab_to, core_to), device_id_type=MESH)

    greet(position, twin)
    for k in range(levels):
        step = 1 << k
        pl.when(jnp.logical_and(level >= k, position + step < slabs))(
            functools.partial(greet, position + step, core)
        )
        pl.when(jnp.logical_and(level >= k, position >= step))(
            functools.partial(greet, position - step, core)
        )

    def turn(value):
        width = value.shape[1] // 2
        return jnp.concatenate([-value[:, width:], value[:, :width]], 1)

    def expand(value):
        return jnp.concatenate([value, turn(value)], 0)

    def adjoint_of(value):
        return jnp.concatenate([value[:, :size].T, -value[:, size:].T], 1)

    def unpack(square):
        turned = square.T
        real = jnp.where(square_row >= square_column, square, turned)
        below = jnp.where(square_row > square_column, -turned, 0.0)
        imag = jnp.where(square_row < square_column, square, below)
        return jnp.concatenate([real, imag], 1)

    def both_halves(block):
        return jnp.concatenate([block[0], block[1]], 1)

    def whole(block):
        return jnp.concatenate([block[0, 0], block[1, 0], block[0, 1], block[1, 1]], 1)

    lane = lax.broadcasted_iota(jnp.int32, (1, 128), 1)
    masked = []
    for plane in range(2):
        rows = []
        for r in range(size // tile):
            blocks = []
            for k in range(size // 128):
                keep = mask_ref[0, r, k * 128 // tile].astype(F32)
                for t in range(1, 128 // tile):
                    other = mask_ref[0, r, k * 128 // tile + t].astype(F32)
                    keep = jnp.where(lane >= t * tile, other, keep)
                piece = factor_ref[0, plane, r * tile : (r + 1) * tile, k * 128 : (k + 1) * 128]
                blocks.append(piece * keep)
            rows.append(jnp.concatenate(blocks, 1))
        masked.append(jnp.concatenate(rows, 0))
    factor = jnp.concatenate(masked, 1)
    bond = dot3(split(factor), pair_map(expand, split(adjoint_of(factor))))
    packed = jnp.where(square_row >= square_column, bond[:, :size], bond[:, size:])
    bond_out[0] = packed[:, :half]
    bond_out[1] = packed[:, half:]

    waves[...] = jnp.concatenate([injection_ref[0, 0], injection_ref[0, 1]], 0).T
    flag[...] = jnp.zeros_like(flag)

    partners = jnp.int32(1)
    for k in range(levels):
        step = 1 << k
        partners += jnp.where(jnp.logical_and(level >= k, position + step < slabs), 1, 0)
        partners += jnp.where(jnp.logical_and(level >= k, position >= step), 1, 0)
    pl.semaphore_wait(barrier, partners)

    def bond_copy():
        return remote(
            bond_out.at[core], bond_in.at[core], send_sem.at[0], bond_sem.at[0], position + 1, core
        )

    pl.when(sends_bond)(lambda: bond_copy().start())

    @pl.when(shallow)
    def _():
        arrival(bond_in.at[core], bond_sem.at[0]).wait_recv()
        join(bond_in.at[core], 0).start()
        own_bond = unpack(both_halves(bond_out))

        @pl.when(position < slabs - 1)
        def _():
            links[1] = own_bond

        @pl.when(position == slabs - 1)
        def _():
            for h in range(2):
                for plane in range(2):
                    first = plane * size + h * half
                    ground[h, plane] += own_bond[:, first : first + half]
            links[1] = jnp.zeros((size, 2 * size), F32)

        join(bond_in.at[twin], 0).wait_recv()
        links[0] = unpack(both_halves(bond_in))

    def add_terms(k, side):
        arrival(terms_in.at[k, side], terms_sem.at[k, side]).wait_recv()
        ground[core] += terms_in[k, side]

    def add_waves(k, side):
        arrival(waves_in.at[k, side], waves_sem.at[k, side]).wait_recv()
        waves[...] += waves_in[k, side, 0:size]
        flag[...] = jnp.maximum(flag[...], waves_in[k, side, size : size + 8])

    def add_waves_level(k):
        pl.when(not_root)(functools.partial(add_waves, k, 0))
        add_waves(k, 1)

    @pl.loop(0, jnp.maximum(level - 1, 0))
    def _(k):
        pl.when(not_root)(functools.partial(add_terms, k, 0))
        add_terms(k, 1)

    pl.when(inner)(lambda: join(ground.at[core], 5).start())

    def link_arrival(side):
        arrival(link_in.at[side, core], link_sem.at[side]).wait_recv()
        join(link_in.at[side, core], 6 + side).start()

    def link_whole(side):
        join(link_in.at[side, twin], 6 + side).wait_recv()
        links[side] = adjoint_of(whole(link_in.at[side]))

    pl.when(deep_left)(functools.partial(link_arrival, 0))
    pl.when(deep)(functools.partial(link_arrival, 1))
    pl.when(deep_left)(functools.partial(link_whole, 0))
    pl.when(deep)(functools.partial(link_whole, 1))

    @pl.loop(0, jnp.maximum(level - 2, 0))
    def _(k):
        add_waves_level(k)

    @pl.when(jnp.logical_not(not_root))
    def _():
        links[0] = jnp.zeros((size, 2 * size), F32)

    pl.when(inner)(lambda: join(ground.at[twin], 5).wait_recv())
    matrix[...] = whole(ground) + links[0] + links[1]

    def corner_arrival(side):
        arrival(corner_in.at[side, core], corner_sem.at[side]).wait_recv()
        join(corner_in.at[side, core], 1 + side).start()

    def corner_whole(side):
        join(corner_in.at[side, twin], 1 + side).wait_recv()
        term = unpack(both_halves(corner_in.at[side]))
        matrix[...] -= term
        links[side] -= term

    pl.when(inner_left)(functools.partial(corner_arrival, 0))
    pl.when(inner)(functools.partial(corner_arrival, 1))
    pl.when(inner_left)(functools.partial(corner_whole, 0))
    pl.when(inner)(functools.partial(corner_whole, 1))

    wide_row = lax.broadcasted_iota(jnp.int32, (size, 2 * size), 0)
    wide_column = lax.broadcasted_iota(jnp.int32, (size, 2 * size), 1)
    unit = jnp.where(wide_row == wide_column, 1.0, 0.0).astype(F32)
    mean = jnp.sum(matrix[...] * unit, keepdims=True) / size
    scale = 1.0 / mean
    scaled = matrix[...] * scale
    power = unit - scaled
    inverse = unit + power
    power = power.astype(BF16)
    power = dot(power, expand(power)).astype(BF16)
    for k in range(3):
        both = dot(jnp.concatenate([inverse.astype(BF16), power], 0), expand(power))
        inverse = inverse + both[:size]
        power = both[size:].astype(BF16)
    inverse = inverse + dot(inverse.astype(BF16), expand(power))
    inverse_pair = split(inverse)
    residual = unit - dot3(split(scaled), pair_map(expand, inverse_pair))
    inverse = inverse + dot3(inverse_pair, pair_map(expand, split(residual)))
    squared = jnp.sum(residual * residual, keepdims=True)
    bad = jnp.where(squared < RESIDUAL_LIMIT, 0.0, 1.0)
    flag[...] = jnp.maximum(flag[...], jnp.broadcast_to(bad, (8, 128)))
    solver = split(inverse * scale)

    def ground_arrival(side):
        arrival(ground_in.at[side, core], ground_sem.at[side]).wait_recv()
        join(ground_in.at[side, core], 3 + side).start()

    def ground_whole(side):
        join(ground_in.at[side, twin], 3 + side).wait_recv()
        links[side] -= whole(ground_in.at[side])
        ground[core] += ground_in[side, core]

    pl.when(inner_left)(functools.partial(ground_arrival, 0))
    pl.when(inner_left)(functools.partial(ground_arrival, 1))
    pl.when(inner)(lambda: join(ground.at[core], 5).wait_send())
    pl.when(inner_left)(functools.partial(ground_whole, 0))
    pl.when(inner_left)(functools.partial(ground_whole, 1))

    @pl.when(jnp.logical_not(has_right))
    def _():
        links[1] = jnp.zeros((size, 2 * size), F32)

    corner_copy = remote(
        corner_out.at[core],
        corner_in.at[far, core],
        send_sem.at[2],
        corner_sem.at[far],
        near_target,
        core,
    )
    ground_copy = remote(
        ground_out, ground_in.at[far, core], send_sem.at[3], ground_sem.at[far], near_target, core
    )
    waves_copy = remote(
        waves_out,
        waves_in.at[level, far],
        send_sem.at[4],
        waves_sem.at[level, far],
        near_target,
        core,
    )
    far_waves_copy = remote(
        far_waves_out,
        waves_in.at[level, near],
        send_sem.at[7],
        waves_sem.at[level, near],
        far_target,
        core,
    )
    far_copy = remote(
        far_out, terms_in.at[level, near], send_sem.at[5], terms_sem.at[level, near], far_target, core
    )
    link_copy = remote(
        link_out, link_in.at[near, core], send_sem.at[6], link_sem.at[near], far_target, core
    )

    def own_half(ref):
        return jnp.concatenate([ref[:, own_real], ref[:, own_imag]], 1)

    def solve_waves():
        @pl.loop(jnp.maximum(level - 2, 0), level)
        def _(k):
            add_waves_level(k)

        solved = dot3(solver, pair_map(expand, split(waves[...])))
        wave_out[0:size] = solved
        return pair_map(expand, split(solved))

    @pl.when(jnp.logical_not(not_root))
    def _():
        solve_waves()

    @pl.when(not_root)
    def _():
        near_adjoint = adjoint_of(links[near])
        near_left = split(near_adjoint)
        solved = dot3(solver, pair_map(expand, split(own_half(links.at[near]))))
        solved_near = pair_map(expand, split(solved))
        product = dot3(near_left, solved_near)
        corner_out[core] = jnp.where(row >= column, product[:, :half], product[:, half:])
        corner_copy.start()
        pl.when(sends_link)(lambda: join(corner_out.at[core], 8).start())

        own_ground = jnp.concatenate([ground[core, 0], ground[core, 1]], 1)
        solved = dot3(solver, pair_map(expand, split(own_ground)))
        solved_ground = pair_map(expand, split(solved))

        product = dot3(near_left, solved_ground)
        ground_out[0] = product[:, :half]
        ground_out[1] = product[:, half:]
        pl.when(sends_ground)(lambda: ground_copy.start())

        @pl.when(sends_link)
        def _():
            join(corner_out.at[twin], 8).wait_recv()
            spare[...] = near_adjoint - unpack(both_halves(corner_out))
            link_out[0] = spare[:, own_real] - ground_out[0]
            link_out[1] = spare[:, own_imag] - ground_out[1]
            link_copy.start()

        far_left = split(adjoint_of(links[far]))

        @pl.when(has_right)
        def _():
            product = dot3(far_left, solved_ground)
            far_out[0] = product[:, :half]
            far_out[1] = product[:, half:]
            far_copy.start()

        solved_waves = solve_waves()
        waves_out[0:size] = dot3(near_left, solved_waves)
        waves_out[size : size + 8] = flag[...]
        waves_copy.start()

        @pl.when(has_right)
        def _():
            far_waves_out[0:size] = dot3(far_left, solved_waves)
            far_waves_out[size : size + 8] = flag[...]
            far_waves_copy.start()

        for side in range(2):
            spike = split(dot3(solver, pair_map(expand, split(links[side]))))
            for part in range(2):
                back[part, :, side * 2 * size : (side + 1) * 2 * size] = spike[part]

    def add_side(side):
        arrival(wave_in.at[side], wave_sem.at[side]).wait_recv()
        pair = pair_map(expand, split(wave_in[side, 0:size]))
        spike = (
            back[0, :, side * 2 * size : (side + 1) * 2 * size],
            back[1, :, side * 2 * size : (side + 1) * 2 * size],
        )
        wave_out[0:size] += dot3(spike, pair)

    @pl.when(not_root)
    def _():
        add_side(0)
        flag[...] = jnp.maximum(flag[...], wave_in[0, size : size + 8])
        pl.when(has_right)(functools.partial(add_side, 1))

    wave_out[size : size + 8] = flag[...]

    @pl.loop(0, level)
    def _(down):
        k = level - 1 - down
        step = jnp.int32(1)
        for m in range(1, levels):
            step = step + jnp.where(k >= m, 1 << (m - 1), 0)
        to_right = remote(
            wave_out, wave_in.at[0], wave_send_sem.at[0], wave_sem.at[0], position + step, core
        )
        to_left = remote(
            wave_out, wave_in.at[1], wave_send_sem.at[1], wave_sem.at[1], position - step, core
        )
        to_right.start()
        pl.when(not_root)(lambda: to_left.start())
        to_right.wait_send()
        pl.when(not_root)(lambda: to_left.wait_send())

    turned_waves = wave_out[0:size].T
    out_ref[0, 0] = turned_waves[:cols]
    out_ref[0, 1] = turned_waves[cols:]
    flag_ref[...] = flag[...]

    pl.when(sends_bond)(lambda: bond_copy().wait_send())
    pl.when(shallow)(lambda: join(bond_in.at[core], 0).wait_send())
    for side in range(2):
        pl.when(deep_left if side == 0 else deep)(
            lambda: join(link_in.at[side, core], 6 + side).wait_send()
        )
        pl.when(inner_left if side == 0 else inner)(
            lambda: join(corner_in.at[side, core], 1 + side).wait_send()
        )
        pl.when(inner_left)(lambda: join(ground_in.at[side, core], 3 + side).wait_send())

    @pl.when(not_root)
    def _():
        corner_copy.wait_send()
        pl.when(sends_ground)(lambda: ground_copy.wait_send())
        waves_copy.wait_send()

        @pl.when(has_right)
        def _():
            far_copy.wait_send()
            far_waves_copy.wait_send()

    @pl.when(sends_link)
    def _():
        join(corner_out.at[core], 8).wait_send()
        link_copy.wait_send()


def tree_path(slabs, bond_factor, tile_mask, potential, injection):
    size = bond_factor.shape[2]
    half = size // 2
    levels = slabs.bit_length() - 1
    vmem = pl.BlockSpec(memory_space=pltpu.VMEM)
    dma = pltpu.SemaphoreType.DMA
    turned = jnp.swapaxes(injection, 2, 3)
    amplitude, flag = pl.pallas_call(
        functools.partial(tree_kernel, slabs),
        out_shape=(
            jax.ShapeDtypeStruct(turned.shape, F32),
            jax.ShapeDtypeStruct((8, 128), F32),
        ),
        in_specs=[vmem, pl.BlockSpec(memory_space=pltpu.SMEM), vmem, vmem],
        out_specs=(vmem, vmem),
        scratch_shapes=[
            pltpu.VMEM((2, 2, size, half), F32),
            pltpu.VMEM((2, size, 2 * size), F32),
            pltpu.VMEM((size, 2 * size), F32),
            pltpu.VMEM((size, 2 * size), F32),
            pltpu.VMEM((size, 128), F32),
            pltpu.VMEM((8, 128), F32),
            pltpu.VMEM((2, size, half), F32),
            pltpu.VMEM((2, size, half), F32),
            pltpu.VMEM((2, size, half), F32),
            pltpu.VMEM((2, 2, size, half), F32),
            pltpu.VMEM((2, size, half), F32),
            pltpu.VMEM((2, 2, 2, size, half), F32),
            pltpu.VMEM((size + 8, 128), F32),
            pltpu.VMEM((size + 8, 128), F32),
            pltpu.VMEM((levels, 2, size + 8, 128), F32),
            pltpu.VMEM((2, size, half), F32),
            pltpu.VMEM((2, 2, 2, size, half), F32),
            pltpu.VMEM((2, size, half), F32),
            pltpu.VMEM((levels, 2, 2, size, half), F32),
            pltpu.VMEM((2, size + 8, 128), F32),
            pltpu.VMEM((size + 8, 128), F32),
            pltpu.VMEM((2, size, 4 * size), BF16),
            dma((8,)),
            dma((1,)),
            dma((2,)),
            dma((2,)),
            dma((levels, 2)),
            dma((2,)),
            dma((levels, 2)),
            dma((2,)),
            dma((2,)),
            dma((9,)),
            dma((9,)),
        ],
        compiler_params=pltpu.CompilerParams(
            collective_id=0, has_side_effects=True, vmem_limit_bytes=52 << 20
        ),
        name="tree_reduction",
    )(bond_factor, tile_mask, potential, turned)
    return jnp.swapaxes(amplitude, 2, 3), flag


def per_device(slabs, bond_factor, tile_mask, potential, injection):
    amplitude, flag = tree_path(slabs, bond_factor, tile_mask, potential, injection)
    return lax.cond(
        flag[0, 0] == 0.0,
        lambda *operands: amplitude,
        direct_path,
        bond_factor,
        tile_mask,
        potential,
        injection,
    )


def solution(mesh):
    in_specs = (
        P("slab", None, None, None),
        P("slab", None, None),
        P("slab", None),
        P("slab", None, None, "rhs"),
    )
    out_specs = P("slab", None, None, "rhs")
    return jax.shard_map(
        functools.partial(per_device, mesh.shape["slab"]),
        mesh=mesh,
        in_specs=in_specs,
        out_specs=out_specs,
        check_vma=False,
    )
```

```python
import functools

import jax
import jax.numpy as jnp
from jax import lax
from jax.experimental import pallas as pl
from jax.experimental.pallas import tpu as pltpu
from jax.sharding import PartitionSpec as P

PRECISE = lax.Precision.HIGHEST
MESH = pl.DeviceIdType.MESH
F32 = jnp.float32
BF16 = jnp.bfloat16
RESIDUAL_LIMIT = 4.0e-4
PARTS = 4


def passed_along(array, axis, by):
    length = lax.axis_size(axis)
    pairs = [(i, i + by) for i in range(length) if 0 <= i + by < length]
    return lax.ppermute(array, axis, pairs)


def matmul_exact(operand, other):
    return jnp.dot(operand, other, precision=PRECISE)


def transposed_product(operand, other):
    return lax.dot_general(operand, other, (((0,), (0,)), ((), ())), precision=PRECISE)


def complex_product(operand, other):
    real_part = matmul_exact(operand[0], other[0]) - matmul_exact(operand[1], other[1])
    imag_part = matmul_exact(operand[0], other[1]) + matmul_exact(operand[1], other[0])
    return jnp.stack([real_part, imag_part])


def adjoint_product(operand, other):
    real_part = transposed_product(operand[0], other[0]) + transposed_product(operand[1], other[1])
    imag_part = transposed_product(operand[0], other[1]) - transposed_product(operand[1], other[0])
    return jnp.stack([real_part, imag_part])


def adjoint(operand):
    return jnp.stack([operand[0].T, -operand[1].T])


def real_form(matrix):
    return jnp.block([[matrix[0], -matrix[1]], [matrix[1], matrix[0]]])


def solve_stacked(factor_low, stacked):
    forward_part = lax.linalg.triangular_solve(factor_low, stacked, left_side=True, lower=True)
    return lax.linalg.triangular_solve(
        factor_low, forward_part, left_side=True, lower=True, transpose_a=True
    )


def direct_path(bond_factor, tile_mask, potential, injection):
    orbitals = bond_factor.shape[2]
    tile_size = orbitals // tile_mask.shape[2]
    slab_total = lax.axis_size("slab")
    position = lax.axis_index("slab")
    core_total = lax.axis_size("rhs")
    core_index = lax.axis_index("rhs")
    half_cols = orbitals // core_total
    pattern = jnp.repeat(jnp.repeat(tile_mask[0], tile_size, 0), tile_size, 1).astype(
        bond_factor.dtype
    )
    factor = bond_factor[0] * pattern[None]
    bond_matrix = complex_product(factor, adjoint(factor))
    previous = passed_along(bond_matrix, "slab", 1)
    onsite = jnp.stack([jnp.diag(potential[0]), jnp.zeros((orbitals, orbitals), potential.dtype)])
    matrix = onsite + bond_matrix + previous
    coupling_up = jnp.where(position == slab_total - 1, jnp.zeros_like(bond_matrix), -bond_matrix)
    coupling_down = -previous
    sources = injection[0]

    def apply_inverse(block, right_side):
        factor_low = jnp.linalg.cholesky(real_form(block))
        stacked = jnp.concatenate([right_side[0], right_side[1]], 0)
        solved = solve_stacked(factor_low, stacked)
        return jnp.stack([solved[:orbitals], solved[orbitals:]])

    def own_columns(block):
        return lax.dynamic_slice_in_dim(block, core_index * half_cols, half_cols, 2)

    levels = slab_total.bit_length() - 1
    for rank_bit in range(levels):
        stride = 1 << rank_bit
        spikes = apply_inverse(
            matrix,
            jnp.concatenate([own_columns(coupling_up), own_columns(coupling_down), sources], 2),
        )
        spike_up = spikes[:, :, :half_cols]
        spike_down = spikes[:, :, half_cols : 2 * half_cols]
        spike_waves = spikes[:, :, 2 * half_cols :]
        toward_upper = adjoint_product(
            coupling_down, jnp.concatenate([spike_down, spike_up, spike_waves], 2)
        )
        from_upper = passed_along(toward_upper, "slab", -stride)
        cross_part = toward_upper[:, :, half_cols : 2 * half_cols]
        toward_lower = adjoint_product(coupling_up, jnp.concatenate([spike_up, spike_waves], 2))
        outgoing = jnp.concatenate(
            [toward_lower[:, :, :half_cols], cross_part, toward_lower[:, :, half_cols:]], 2
        )
        from_lower = passed_along(outgoing, "slab", stride)
        diag_change = from_upper[:, :, :half_cols] + from_lower[:, :, :half_cols]
        new_up = -from_upper[:, :, half_cols : 2 * half_cols]
        coupling_new = from_lower[:, :, half_cols : 2 * half_cols]
        sources = sources - from_upper[:, :, 2 * half_cols :] - from_lower[:, :, 2 * half_cols :]
        gathered = (
            lax.all_gather(diag_change, "rhs", axis=2, tiled=True),
            lax.all_gather(new_up, "rhs", axis=2, tiled=True),
            lax.all_gather(coupling_new, "rhs", axis=2, tiled=True),
        )
        matrix = matrix - gathered[0]
        coupling_up = gathered[1]
        coupling_down = -adjoint(gathered[2])
    amplitude = apply_inverse(matrix, sources)
    return amplitude[None]


def split(value):
    high = value.astype(BF16)
    low = (value - high.astype(F32)).astype(BF16)
    return high, low


def dot(left, right):
    return jnp.dot(left, right, preferred_element_type=F32)


def dot3(left, right):
    high = dot(left[0], right[0])
    return high + (dot(left[0], right[1]) + dot(left[1], right[0]))


def pair_map(function, pair):
    return function(pair[0]), function(pair[1])


def tree_kernel(
    slabs,
    factor_ref,
    mask_ref,
    potential_ref,
    injection_ref,
    out_ref,
    flag_ref,
    ground,
    links,
    matrix,
    spare,
    waves,
    flag,
    bond_out,
    bond_in,
    corner_out,
    corner_in,
    ground_out,
    ground_in,
    waves_out,
    far_waves_out,
    waves_in,
    link_out,
    link_in,
    far_out,
    terms_in,
    wave_in,
    wave_out,
    back,
    send_sem,
    bond_sem,
    corner_sem,
    ground_sem,
    waves_sem,
    link_sem,
    terms_sem,
    wave_sem,
    wave_send_sem,
    join_send_sem,
    join_sem,
):
    size = factor_ref.shape[2]
    half = size // 2
    cols = injection_ref.shape[2]
    part_cols = cols // PARTS
    part_width = 2 * part_cols
    part_rows = size // PARTS
    tile = size // mask_ref.shape[2]
    position = lax.axis_index("slab")
    core = lax.axis_index("rhs")
    twin = 1 - core
    levels = slabs.bit_length() - 1

    level = jnp.int32(0)
    stride = jnp.int32(1)
    for k in range(1, levels + 1):
        even = jnp.where(position % (1 << k) == 0, 1, 0)
        level = level + even
        stride = stride + even * (1 << (k - 1))
    not_root = position > 0
    inner = level > 0
    inner_left = jnp.logical_and(inner, not_root)
    deep = level > 1
    deep_left = jnp.logical_and(deep, not_root)
    shallow = position % 4 != 0
    has_right = jnp.logical_and(not_root, position + stride < slabs)
    near_is_right = jnp.logical_and(has_right, (position // stride) % 4 == 1)
    near = jnp.where(near_is_right, 1, 0)
    far = 1 - near
    near_target = jnp.where(near_is_right, position + stride, position - stride)
    far_target = jnp.where(near_is_right, position - stride, position + stride)
    near_is_root = near_target == 0
    sends_ground = jnp.logical_and(not_root, jnp.logical_not(near_is_root))
    sends_link = jnp.logical_and(
        has_right, jnp.logical_or((far_target // stride) % 8 == 4, jnp.logical_and(far_target == 0, stride * 4 == slabs))
    )
    sends_bond = (position + 1) % 4 != 0

    def remote(source, target, sent, received, slab_to, core_to):
        return pltpu.make_async_remote_copy(
            src_ref=source,
            dst_ref=target,
            send_sem=sent,
            recv_sem=received,
            device_id=(slab_to, core_to),
            device_id_type=MESH,
        )

    def arrival(block, received):
        return remote(block, block, send_sem.at[1], received, position, twin)

    def join(block, which):
        return remote(block, block, join_send_sem.at[which], join_sem.at[which], position, twin)

    row = lax.broadcasted_iota(jnp.int32, (size, half), 0)
    lane_half = lax.broadcasted_iota(jnp.int32, (size, half), 1)
    column = lane_half + core * half
    square_row = lax.broadcasted_iota(jnp.int32, (size, size), 0)
    square_column = lax.broadcasted_iota(jnp.int32, (size, size), 1)
    own_real = pl.ds(pl.multiple_of(core * half, half), half)
    own_imag = pl.ds(pl.multiple_of(core * half + size, half), half)

    for h in range(2):
        energies = jnp.broadcast_to(potential_ref[:, h * half : (h + 1) * half], (size, half))
        ground[h, 0] = jnp.where(row == lane_half + h * half, energies, 0.0)
        ground[h, 1] = jnp.zeros((size, half), F32)

    barrier = pltpu.get_barrier_semaphore()

    def greet(slab_to, core_to):
        pl.semaphore_signal(barrier, inc=1, device_id=(slab_to, core_to), device_id_type=MESH)

    greet(position, twin)
    for k in range(levels):
        step = 1 << k
        pl.when(jnp.logical_and(level >= k, position + step < slabs))(
            functools.partial(greet, position + step, core)
        )
        pl.when(jnp.logical_and(level >= k, position >= step))(
            functools.partial(greet, position - step, core)
        )

    def turn(value):
        width = value.shape[1] // 2
        return jnp.concatenate([-value[:, width:], value[:, :width]], 1)

    def expand(value):
        return jnp.concatenate([value, turn(value)], 0)

    def adjoint_of(value):
        return jnp.concatenate([value[:, :size].T, -value[:, size:].T], 1)

    def unpack(square):
        turned = square.T
        real = jnp.where(square_row >= square_column, square, turned)
        below = jnp.where(square_row > square_column, -turned, 0.0)
        imag = jnp.where(square_row < square_column, square, below)
        return jnp.concatenate([real, imag], 1)

    def both_halves(block):
        return jnp.concatenate([block[0], block[1]], 1)

    def whole(block):
        return jnp.concatenate([block[0, 0], block[1, 0], block[0, 1], block[1, 1]], 1)

    lane = lax.broadcasted_iota(jnp.int32, (1, 128), 1)
    masked = []
    for plane in range(2):
        rows = []
        for r in range(size // tile):
            blocks = []
            for k in range(size // 128):
                keep = mask_ref[0, r, k * 128 // tile].astype(F32)
                for t in range(1, 128 // tile):
                    other = mask_ref[0, r, k * 128 // tile + t].astype(F32)
                    keep = jnp.where(lane >= t * tile, other, keep)
                piece = factor_ref[0, plane, r * tile : (r + 1) * tile, k * 128 : (k + 1) * 128]
                blocks.append(piece * keep)
            rows.append(jnp.concatenate(blocks, 1))
        masked.append(jnp.concatenate(rows, 0))
    factor = jnp.concatenate(masked, 1)
    bond = dot3(split(factor), pair_map(expand, split(adjoint_of(factor))))
    packed = jnp.where(square_row >= square_column, bond[:, :size], bond[:, size:])
    bond_out[0] = packed[:, :half]
    bond_out[1] = packed[:, half:]

    waves[...] = jnp.concatenate(
        [
            injection_ref[0, plane, p * part_cols : (p + 1) * part_cols]
            for p in range(PARTS)
            for plane in range(2)
        ],
        0,
    ).T
    flag[...] = jnp.zeros_like(flag)

    partners = jnp.int32(1)
    for k in range(levels):
        step = 1 << k
        partners += jnp.where(jnp.logical_and(level >= k, position + step < slabs), 1, 0)
        partners += jnp.where(jnp.logical_and(level >= k, position >= step), 1, 0)
    pl.semaphore_wait(barrier, partners)

    def bond_copy():
        return remote(
            bond_out.at[core], bond_in.at[core], send_sem.at[0], bond_sem.at[0], position + 1, core
        )

    pl.when(sends_bond)(lambda: bond_copy().start())

    @pl.when(shallow)
    def _():
        arrival(bond_in.at[core], bond_sem.at[0]).wait_recv()
        join(bond_in.at[core], 0).start()
        own_bond = unpack(both_halves(bond_out))

        @pl.when(position < slabs - 1)
        def _():
            links[1] = own_bond

        @pl.when(position == slabs - 1)
        def _():
            for h in range(2):
                for plane in range(2):
                    first = plane * size + h * half
                    ground[h, plane] += own_bond[:, first : first + half]
            links[1] = jnp.zeros((size, 2 * size), F32)

        join(bond_in.at[twin], 0).wait_recv()
        links[0] = unpack(both_halves(bond_in))

    def add_terms(k, side):
        arrival(terms_in.at[k, side], terms_sem.at[k, side]).wait_recv()
        ground[core] += terms_in[k, side]

    def add_waves(k, side):
        arrival(waves_in.at[k, side], waves_sem.at[k, side]).wait_recv()
        waves[...] += waves_in[k, side, 0:size]
        flag[...] = jnp.maximum(flag[...], waves_in[k, side, size : size + 8])

    def add_waves_level(k):
        pl.when(not_root)(functools.partial(add_waves, k, 0))
        add_waves(k, 1)

    @pl.loop(0, jnp.maximum(level - 1, 0))
    def _(k):
        pl.when(not_root)(functools.partial(add_terms, k, 0))
        add_terms(k, 1)

    pl.when(inner)(lambda: join(ground.at[core], 5).start())

    def link_arrival(side):
        arrival(link_in.at[side, core], link_sem.at[side]).wait_recv()
        join(link_in.at[side, core], 6 + side).start()

    def link_whole(side):
        join(link_in.at[side, twin], 6 + side).wait_recv()
        links[side] = adjoint_of(whole(link_in.at[side]))

    pl.when(deep_left)(functools.partial(link_arrival, 0))
    pl.when(deep)(functools.partial(link_arrival, 1))
    pl.when(deep_left)(functools.partial(link_whole, 0))
    pl.when(deep)(functools.partial(link_whole, 1))

    @pl.loop(0, jnp.maximum(level - 2, 0))
    def _(k):
        add_waves_level(k)

    @pl.when(jnp.logical_not(not_root))
    def _():
        links[0] = jnp.zeros((size, 2 * size), F32)

    pl.when(inner)(lambda: join(ground.at[twin], 5).wait_recv())
    matrix[...] = whole(ground) + links[0] + links[1]

    def corner_arrival(side):
        arrival(corner_in.at[side, core], corner_sem.at[side]).wait_recv()
        join(corner_in.at[side, core], 1 + side).start()

    def corner_whole(side):
        join(corner_in.at[side, twin], 1 + side).wait_recv()
        term = unpack(both_halves(corner_in.at[side]))
        matrix[...] -= term
        links[side] -= term

    pl.when(inner_left)(functools.partial(corner_arrival, 0))
    pl.when(inner)(functools.partial(corner_arrival, 1))
    pl.when(inner_left)(functools.partial(corner_whole, 0))
    pl.when(inner)(functools.partial(corner_whole, 1))

    wide_row = lax.broadcasted_iota(jnp.int32, (size, 2 * size), 0)
    wide_column = lax.broadcasted_iota(jnp.int32, (size, 2 * size), 1)
    unit = jnp.where(wide_row == wide_column, 1.0, 0.0).astype(F32)
    mean = jnp.sum(matrix[...] * unit, keepdims=True) / size
    scale = 1.0 / mean
    scaled = matrix[...] * scale
    power = unit - scaled
    inverse = unit + power
    power = power.astype(BF16)
    power = dot(power, expand(power)).astype(BF16)
    for k in range(3):
        both = dot(jnp.concatenate([inverse.astype(BF16), power], 0), expand(power))
        inverse = inverse + both[:size]
        power = both[size:].astype(BF16)
    inverse = inverse + dot(inverse.astype(BF16), expand(power))
    inverse_pair = split(inverse)
    residual = unit - dot3(split(scaled), pair_map(expand, inverse_pair))
    inverse = inverse + dot3(inverse_pair, pair_map(expand, split(residual)))
    squared = jnp.sum(residual * residual, keepdims=True)
    bad = jnp.where(squared < RESIDUAL_LIMIT, 0.0, 1.0)
    flag[...] = jnp.maximum(flag[...], jnp.broadcast_to(bad, (8, 128)))
    solver = split(inverse * scale)

    def ground_arrival(side):
        arrival(ground_in.at[side, core], ground_sem.at[side]).wait_recv()
        join(ground_in.at[side, core], 3 + side).start()

    def ground_whole(side):
        join(ground_in.at[side, twin], 3 + side).wait_recv()
        links[side] -= whole(ground_in.at[side])
        ground[core] += ground_in[side, core]

    pl.when(inner_left)(functools.partial(ground_arrival, 0))
    pl.when(inner_left)(functools.partial(ground_arrival, 1))
    pl.when(inner)(lambda: join(ground.at[core], 5).wait_send())
    pl.when(inner_left)(functools.partial(ground_whole, 0))
    pl.when(inner_left)(functools.partial(ground_whole, 1))

    @pl.when(jnp.logical_not(has_right))
    def _():
        links[1] = jnp.zeros((size, 2 * size), F32)
        wave_in[1] = jnp.zeros(wave_in.shape[1:], F32)

    corner_copy = remote(
        corner_out.at[core],
        corner_in.at[far, core],
        send_sem.at[2],
        corner_sem.at[far],
        near_target,
        core,
    )
    ground_copy = remote(
        ground_out, ground_in.at[far, core], send_sem.at[3], ground_sem.at[far], near_target, core
    )
    waves_copy = remote(
        waves_out,
        waves_in.at[level, far],
        send_sem.at[4],
        waves_sem.at[level, far],
        near_target,
        core,
    )
    far_waves_copy = remote(
        far_waves_out,
        waves_in.at[level, near],
        send_sem.at[7],
        waves_sem.at[level, near],
        far_target,
        core,
    )
    far_copy = remote(
        far_out, terms_in.at[level, near], send_sem.at[5], terms_sem.at[level, near], far_target, core
    )
    link_copy = remote(
        link_out, link_in.at[near, core], send_sem.at[6], link_sem.at[near], far_target, core
    )

    def own_half(ref):
        return jnp.concatenate([ref[:, own_real], ref[:, own_imag]], 1)

    def turn_waves(value):
        swapped = jnp.where(
            lane % part_width < part_cols,
            -pltpu.roll(value, 128 - part_cols, 1),
            pltpu.roll(value, part_cols, 1),
        )
        return jnp.concatenate([value, swapped], 0)

    def expand_waves(value):
        high, low = split(value)
        high_wide, low_wide = high.astype(F32), low.astype(F32)
        return turn_waves(high_wide).astype(BF16), turn_waves(low_wide).astype(BF16)

    def pack_part(value):
        packed_part = value[0:part_rows]
        for q in range(1, PARTS):
            shifted = pltpu.roll(value[q * part_rows : (q + 1) * part_rows], q * part_width, 1)
            packed_part = jnp.where(lane >= q * part_width, shifted, packed_part)
        return packed_part

    def unpack_part(value):
        pieces = [value]
        for q in range(1, PARTS):
            pieces.append(pltpu.roll(value, 128 - q * part_width, 1))
        return jnp.concatenate(pieces, 0)

    def solve_waves():
        @pl.loop(jnp.maximum(level - 2, 0), level)
        def _(k):
            add_waves_level(k)

        solved = dot3(solver, expand_waves(waves[...]))
        waves[...] = solved
        return expand_waves(solved)

    @pl.when(jnp.logical_not(not_root))
    def _():
        solve_waves()

    @pl.when(not_root)
    def _():
        near_adjoint = adjoint_of(links[near])
        near_left = split(near_adjoint)
        solved = dot3(solver, pair_map(expand, split(own_half(links.at[near]))))
        solved_near = pair_map(expand, split(solved))
        product = dot3(near_left, solved_near)
        corner_out[core] = jnp.where(row >= column, product[:, :half], product[:, half:])
        corner_copy.start()
        pl.when(sends_link)(lambda: join(corner_out.at[core], 8).start())

        own_ground = jnp.concatenate([ground[core, 0], ground[core, 1]], 1)
        solved = dot3(solver, pair_map(expand, split(own_ground)))
        solved_ground = pair_map(expand, split(solved))

        product = dot3(near_left, solved_ground)
        ground_out[0] = product[:, :half]
        ground_out[1] = product[:, half:]
        pl.when(sends_ground)(lambda: ground_copy.start())

        @pl.when(sends_link)
        def _():
            join(corner_out.at[twin], 8).wait_recv()
            spare[...] = near_adjoint - unpack(both_halves(corner_out))
            link_out[0] = spare[:, own_real] - ground_out[0]
            link_out[1] = spare[:, own_imag] - ground_out[1]
            link_copy.start()

        far_left = split(adjoint_of(links[far]))

        @pl.when(has_right)
        def _():
            product = dot3(far_left, solved_ground)
            far_out[0] = product[:, :half]
            far_out[1] = product[:, half:]
            far_copy.start()

        solved_waves = solve_waves()
        waves_out[0:size] = dot3(near_left, solved_waves)
        waves_out[size : size + 8] = flag[...]
        waves_copy.start()

        @pl.when(has_right)
        def _():
            far_waves_out[0:size] = dot3(far_left, solved_waves)
            far_waves_out[size : size + 8] = flag[...]
            far_waves_copy.start()

        for side in range(2):
            spike = split(dot3(solver, pair_map(expand, split(links[side]))))
            for part in range(2):
                back[part, :, side * 2 * size : (side + 1) * 2 * size] = spike[part]

    def wave_sends(k, step, p):
        to_right = remote(
            wave_out.at[p], wave_in.at[0, p], wave_send_sem.at[0, p], wave_sem.at[0, p], position + step, core
        )
        to_left = remote(
            wave_out.at[p], wave_in.at[1, p], wave_send_sem.at[1, p], wave_sem.at[1, p], position - step, core
        )
        return to_right, to_left

    def start_waves(k, step, p):
        to_right, to_left = wave_sends(k, step, p)
        to_right.start()
        pl.when(not_root)(lambda: to_left.start())

    def finish_waves(k, step, p):
        to_right, to_left = wave_sends(k, step, p)
        to_right.wait_send()
        pl.when(not_root)(lambda: to_left.wait_send())

    first_step = jnp.where(inner, stride // 2, 1)
    rows_flag = pl.ds(part_rows, 8)
    for p in range(PARTS):
        own = pltpu.roll(waves[...], 128 - p * part_width, 1) if p else waves[...]
        wave_out[p, 0:part_rows] = pack_part(own)

        @pl.when(not_root)
        def _():
            arrival(wave_in.at[0, p], wave_sem.at[0, p]).wait_recv()
            pl.when(has_right)(lambda: arrival(wave_in.at[1, p], wave_sem.at[1, p]).wait_recv())
            sides = [expand_waves(unpack_part(wave_in[side, p, 0:part_rows])) for side in range(2)]
            pair = [jnp.concatenate([sides[0][e], sides[1][e]], 0) for e in range(2)]
            total = dot3((back[0], back[1]), pair)
            wave_out[p, 0:part_rows] += pack_part(total)
            if p == 0:
                flag[...] = jnp.maximum(flag[...], wave_in[0, 0, rows_flag])

        wave_out[p, rows_flag] = flag[...]
        pl.when(inner)(functools.partial(start_waves, level - 1, first_step, p))

    @pl.when(inner)
    def _():
        for p in range(PARTS):
            finish_waves(level - 1, first_step, p)

    @pl.loop(1, level)
    def _(down):
        k = level - 1 - down
        step = jnp.int32(1)
        for m in range(1, levels):
            step = step + jnp.where(k >= m, 1 << (m - 1), 0)
        for p in range(PARTS):
            start_waves(k, step, p)
        for p in range(PARTS):
            finish_waves(k, step, p)

    turned_waves = jnp.concatenate(
        [unpack_part(wave_out[p, 0:part_rows])[:, :part_width] for p in range(PARTS)], 1
    ).T
    for p in range(PARTS):
        for plane in range(2):
            first = p * part_width + plane * part_cols
            out_ref[0, plane, p * part_cols : (p + 1) * part_cols] = turned_waves[first : first + part_cols]
    flag_ref[...] = flag[...]

    pl.when(sends_bond)(lambda: bond_copy().wait_send())
    pl.when(shallow)(lambda: join(bond_in.at[core], 0).wait_send())
    for side in range(2):
        pl.when(deep_left if side == 0 else deep)(
            lambda: join(link_in.at[side, core], 6 + side).wait_send()
        )
        pl.when(inner_left if side == 0 else inner)(
            lambda: join(corner_in.at[side, core], 1 + side).wait_send()
        )
        pl.when(inner_left)(lambda: join(ground_in.at[side, core], 3 + side).wait_send())

    @pl.when(not_root)
    def _():
        corner_copy.wait_send()
        pl.when(sends_ground)(lambda: ground_copy.wait_send())
        waves_copy.wait_send()

        @pl.when(has_right)
        def _():
            far_copy.wait_send()
            far_waves_copy.wait_send()

    @pl.when(sends_link)
    def _():
        join(corner_out.at[core], 8).wait_send()
        link_copy.wait_send()


def tree_path(slabs, bond_factor, tile_mask, potential, injection):
    size = bond_factor.shape[2]
    half = size // 2
    levels = slabs.bit_length() - 1
    vmem = pl.BlockSpec(memory_space=pltpu.VMEM)
    dma = pltpu.SemaphoreType.DMA
    turned = jnp.swapaxes(injection, 2, 3)
    amplitude, flag = pl.pallas_call(
        functools.partial(tree_kernel, slabs),
        out_shape=(
            jax.ShapeDtypeStruct(turned.shape, F32),
            jax.ShapeDtypeStruct((8, 128), F32),
        ),
        in_specs=[vmem, pl.BlockSpec(memory_space=pltpu.SMEM), vmem, vmem],
        out_specs=(vmem, vmem),
        scratch_shapes=[
            pltpu.VMEM((2, 2, size, half), F32),
            pltpu.VMEM((2, size, 2 * size), F32),
            pltpu.VMEM((size, 2 * size), F32),
            pltpu.VMEM((size, 2 * size), F32),
            pltpu.VMEM((size, 128), F32),
            pltpu.VMEM((8, 128), F32),
            pltpu.VMEM((2, size, half), F32),
            pltpu.VMEM((2, size, half), F32),
            pltpu.VMEM((2, size, half), F32),
            pltpu.VMEM((2, 2, size, half), F32),
            pltpu.VMEM((2, size, half), F32),
            pltpu.VMEM((2, 2, 2, size, half), F32),
            pltpu.VMEM((size + 8, 128), F32),
            pltpu.VMEM((size + 8, 128), F32),
            pltpu.VMEM((levels, 2, size + 8, 128), F32),
            pltpu.VMEM((2, size, half), F32),
            pltpu.VMEM((2, 2, 2, size, half), F32),
            pltpu.VMEM((2, size, half), F32),
            pltpu.VMEM((levels, 2, 2, size, half), F32),
            pltpu.VMEM((2, PARTS, size // PARTS + 8, 128), F32),
            pltpu.VMEM((PARTS, size // PARTS + 8, 128), F32),
            pltpu.VMEM((2, size, 4 * size), BF16),
            dma((8,)),
            dma((1,)),
            dma((2,)),
            dma((2,)),
            dma((levels, 2)),
            dma((2,)),
            dma((levels, 2)),
            dma((2, PARTS)),
            dma((2, PARTS)),
            dma((9,)),
            dma((9,)),
        ],
        compiler_params=pltpu.CompilerParams(
            collective_id=0, has_side_effects=True, vmem_limit_bytes=52 << 20
        ),
        name="tree_reduction",
    )(bond_factor, tile_mask, potential, turned)
    return jnp.swapaxes(amplitude, 2, 3), flag


def per_device(slabs, bond_factor, tile_mask, potential, injection):
    amplitude, flag = tree_path(slabs, bond_factor, tile_mask, potential, injection)
    return lax.cond(
        flag[0, 0] == 0.0,
        lambda *operands: amplitude,
        direct_path,
        bond_factor,
        tile_mask,
        potential,
        injection,
    )


def solution(mesh):
    in_specs = (
        P("slab", None, None, None),
        P("slab", None, None),
        P("slab", None),
        P("slab", None, None, "rhs"),
    )
    out_specs = P("slab", None, None, "rhs")
    return jax.shard_map(
        functools.partial(per_device, mesh.shape["slab"]),
        mesh=mesh,
        in_specs=in_specs,
        out_specs=out_specs,
        check_vma=False,
    )
```

```python
import functools

import jax
import jax.numpy as jnp
from jax import lax
from jax.experimental import pallas as pl
from jax.experimental.pallas import tpu as pltpu
from jax.sharding import PartitionSpec as P

PRECISE = lax.Precision.HIGHEST
MESH = pl.DeviceIdType.MESH
F32 = jnp.float32
BF16 = jnp.bfloat16
RESIDUAL_LIMIT = 4.0e-4
PARTS = 4


def passed_along(array, axis, by):
    length = lax.axis_size(axis)
    pairs = [(i, i + by) for i in range(length) if 0 <= i + by < length]
    return lax.ppermute(array, axis, pairs)


def matmul_exact(operand, other):
    return jnp.dot(operand, other, precision=PRECISE)


def transposed_product(operand, other):
    return lax.dot_general(operand, other, (((0,), (0,)), ((), ())), precision=PRECISE)


def complex_product(operand, other):
    real_part = matmul_exact(operand[0], other[0]) - matmul_exact(operand[1], other[1])
    imag_part = matmul_exact(operand[0], other[1]) + matmul_exact(operand[1], other[0])
    return jnp.stack([real_part, imag_part])


def adjoint_product(operand, other):
    real_part = transposed_product(operand[0], other[0]) + transposed_product(operand[1], other[1])
    imag_part = transposed_product(operand[0], other[1]) - transposed_product(operand[1], other[0])
    return jnp.stack([real_part, imag_part])


def adjoint(operand):
    return jnp.stack([operand[0].T, -operand[1].T])


def real_form(matrix):
    return jnp.block([[matrix[0], -matrix[1]], [matrix[1], matrix[0]]])


def solve_stacked(factor_low, stacked):
    forward_part = lax.linalg.triangular_solve(factor_low, stacked, left_side=True, lower=True)
    return lax.linalg.triangular_solve(
        factor_low, forward_part, left_side=True, lower=True, transpose_a=True
    )


def direct_path(bond_factor, tile_mask, potential, injection):
    orbitals = bond_factor.shape[2]
    tile_size = orbitals // tile_mask.shape[2]
    slab_total = lax.axis_size("slab")
    position = lax.axis_index("slab")
    core_total = lax.axis_size("rhs")
    core_index = lax.axis_index("rhs")
    half_cols = orbitals // core_total
    pattern = jnp.repeat(jnp.repeat(tile_mask[0], tile_size, 0), tile_size, 1).astype(
        bond_factor.dtype
    )
    factor = bond_factor[0] * pattern[None]
    bond_matrix = complex_product(factor, adjoint(factor))
    previous = passed_along(bond_matrix, "slab", 1)
    onsite = jnp.stack([jnp.diag(potential[0]), jnp.zeros((orbitals, orbitals), potential.dtype)])
    matrix = onsite + bond_matrix + previous
    coupling_up = jnp.where(position == slab_total - 1, jnp.zeros_like(bond_matrix), -bond_matrix)
    coupling_down = -previous
    sources = injection[0]

    def apply_inverse(block, right_side):
        factor_low = jnp.linalg.cholesky(real_form(block))
        stacked = jnp.concatenate([right_side[0], right_side[1]], 0)
        solved = solve_stacked(factor_low, stacked)
        return jnp.stack([solved[:orbitals], solved[orbitals:]])

    def own_columns(block):
        return lax.dynamic_slice_in_dim(block, core_index * half_cols, half_cols, 2)

    levels = slab_total.bit_length() - 1
    for rank_bit in range(levels):
        stride = 1 << rank_bit
        spikes = apply_inverse(
            matrix,
            jnp.concatenate([own_columns(coupling_up), own_columns(coupling_down), sources], 2),
        )
        spike_up = spikes[:, :, :half_cols]
        spike_down = spikes[:, :, half_cols : 2 * half_cols]
        spike_waves = spikes[:, :, 2 * half_cols :]
        toward_upper = adjoint_product(
            coupling_down, jnp.concatenate([spike_down, spike_up, spike_waves], 2)
        )
        from_upper = passed_along(toward_upper, "slab", -stride)
        cross_part = toward_upper[:, :, half_cols : 2 * half_cols]
        toward_lower = adjoint_product(coupling_up, jnp.concatenate([spike_up, spike_waves], 2))
        outgoing = jnp.concatenate(
            [toward_lower[:, :, :half_cols], cross_part, toward_lower[:, :, half_cols:]], 2
        )
        from_lower = passed_along(outgoing, "slab", stride)
        diag_change = from_upper[:, :, :half_cols] + from_lower[:, :, :half_cols]
        new_up = -from_upper[:, :, half_cols : 2 * half_cols]
        coupling_new = from_lower[:, :, half_cols : 2 * half_cols]
        sources = sources - from_upper[:, :, 2 * half_cols :] - from_lower[:, :, 2 * half_cols :]
        gathered = (
            lax.all_gather(diag_change, "rhs", axis=2, tiled=True),
            lax.all_gather(new_up, "rhs", axis=2, tiled=True),
            lax.all_gather(coupling_new, "rhs", axis=2, tiled=True),
        )
        matrix = matrix - gathered[0]
        coupling_up = gathered[1]
        coupling_down = -adjoint(gathered[2])
    amplitude = apply_inverse(matrix, sources)
    return amplitude[None]


def split(value):
    high = value.astype(BF16)
    low = (value - high.astype(F32)).astype(BF16)
    return high, low


def dot(left, right):
    return jnp.dot(left, right, preferred_element_type=F32)


def dot3(left, right):
    high = dot(left[0], right[0])
    return high + (dot(left[0], right[1]) + dot(left[1], right[0]))


def pair_map(function, pair):
    return function(pair[0]), function(pair[1])


def tree_kernel(
    slabs,
    factor_ref,
    mask_ref,
    potential_ref,
    injection_ref,
    out_ref,
    flag_ref,
    ground,
    links,
    matrix,
    spare,
    waves,
    flag,
    bond_out,
    bond_in,
    corner_out,
    corner_in,
    ground_out,
    ground_in,
    waves_out,
    far_waves_out,
    waves_in,
    link_out,
    link_in,
    far_out,
    terms_in,
    wave_in,
    wave_out,
    back,
    send_sem,
    bond_sem,
    corner_sem,
    ground_sem,
    waves_sem,
    link_sem,
    terms_sem,
    wave_sem,
    wave_send_sem,
    join_send_sem,
    join_sem,
):
    size = factor_ref.shape[2]
    half = size // 2
    cols = injection_ref.shape[2]
    part_cols = cols // PARTS
    part_width = 2 * part_cols
    part_rows = size // PARTS
    tile = size // mask_ref.shape[2]
    position = lax.axis_index("slab")
    core = lax.axis_index("rhs")
    twin = 1 - core
    levels = slabs.bit_length() - 1

    level = jnp.int32(0)
    stride = jnp.int32(1)
    for k in range(1, levels + 1):
        even = jnp.where(position % (1 << k) == 0, 1, 0)
        level = level + even
        stride = stride + even * (1 << (k - 1))
    not_root = position > 0
    inner = level > 0
    inner_left = jnp.logical_and(inner, not_root)
    deep = level > 1
    deep_left = jnp.logical_and(deep, not_root)
    shallow = position % 4 != 0
    has_right = jnp.logical_and(not_root, position + stride < slabs)
    near_is_right = jnp.logical_and(has_right, (position // stride) % 4 == 1)
    near = jnp.where(near_is_right, 1, 0)
    far = 1 - near
    near_target = jnp.where(near_is_right, position + stride, position - stride)
    far_target = jnp.where(near_is_right, position - stride, position + stride)
    near_is_root = near_target == 0
    sends_ground = jnp.logical_and(not_root, jnp.logical_not(near_is_root))
    sends_link = jnp.logical_and(
        has_right, jnp.logical_or((far_target // stride) % 8 == 4, jnp.logical_and(far_target == 0, stride * 4 == slabs))
    )
    sends_bond = (position + 1) % 4 != 0

    def remote(source, target, sent, received, slab_to, core_to):
        return pltpu.make_async_remote_copy(
            src_ref=source,
            dst_ref=target,
            send_sem=sent,
            recv_sem=received,
            device_id=(slab_to, core_to),
            device_id_type=MESH,
        )

    def arrival(block, received):
        return remote(block, block, send_sem.at[1], received, position, twin)

    def join(block, which):
        return remote(block, block, join_send_sem.at[which], join_sem.at[which], position, twin)

    row = lax.broadcasted_iota(jnp.int32, (size, half), 0)
    lane_half = lax.broadcasted_iota(jnp.int32, (size, half), 1)
    column = lane_half + core * half
    square_row = lax.broadcasted_iota(jnp.int32, (size, size), 0)
    square_column = lax.broadcasted_iota(jnp.int32, (size, size), 1)
    own_real = pl.ds(pl.multiple_of(core * half, half), half)
    own_imag = pl.ds(pl.multiple_of(core * half + size, half), half)

    for h in range(2):
        energies = jnp.broadcast_to(potential_ref[:, h * half : (h + 1) * half], (size, half))
        ground[h, 0] = jnp.where(row == lane_half + h * half, energies, 0.0)
        ground[h, 1] = jnp.zeros((size, half), F32)

    barrier = pltpu.get_barrier_semaphore()

    def greet(slab_to, core_to):
        pl.semaphore_signal(barrier, inc=1, device_id=(slab_to, core_to), device_id_type=MESH)

    greet(position, twin)
    for k in range(levels):
        step = 1 << k
        pl.when(jnp.logical_and(level >= k, position + step < slabs))(
            functools.partial(greet, position + step, core)
        )
        pl.when(jnp.logical_and(level >= k, position >= step))(
            functools.partial(greet, position - step, core)
        )

    def turn(value):
        width = value.shape[1] // 2
        return jnp.concatenate([-value[:, width:], value[:, :width]], 1)

    def expand(value):
        return jnp.concatenate([value, turn(value)], 0)

    def adjoint_of(value):
        return jnp.concatenate([value[:, :size].T, -value[:, size:].T], 1)

    def unpack(square):
        turned = square.T
        real = jnp.where(square_row >= square_column, square, turned)
        below = jnp.where(square_row > square_column, -turned, 0.0)
        imag = jnp.where(square_row < square_column, square, below)
        return jnp.concatenate([real, imag], 1)

    def both_halves(block):
        return jnp.concatenate([block[0], block[1]], 1)

    def whole(block):
        return jnp.concatenate([block[0, 0], block[1, 0], block[0, 1], block[1, 1]], 1)

    lane = lax.broadcasted_iota(jnp.int32, (1, 128), 1)
    masked = []
    for plane in range(2):
        rows = []
        for r in range(size // tile):
            blocks = []
            for k in range(size // 128):
                keep = mask_ref[0, r, k * 128 // tile].astype(F32)
                for t in range(1, 128 // tile):
                    other = mask_ref[0, r, k * 128 // tile + t].astype(F32)
                    keep = jnp.where(lane >= t * tile, other, keep)
                piece = factor_ref[0, plane, r * tile : (r + 1) * tile, k * 128 : (k + 1) * 128]
                blocks.append(piece * keep)
            rows.append(jnp.concatenate(blocks, 1))
        masked.append(jnp.concatenate(rows, 0))
    factor = jnp.concatenate(masked, 1)
    bond = dot3(split(factor), pair_map(expand, split(adjoint_of(factor))))
    packed = jnp.where(square_row >= square_column, bond[:, :size], bond[:, size:])
    bond_out[0] = packed[:, :half]
    bond_out[1] = packed[:, half:]

    waves[...] = jnp.concatenate(
        [
            injection_ref[0, plane, p * part_cols : (p + 1) * part_cols]
            for p in range(PARTS)
            for plane in range(2)
        ],
        0,
    ).T
    flag[...] = jnp.zeros_like(flag)

    partners = jnp.int32(1)
    for k in range(levels):
        step = 1 << k
        partners += jnp.where(jnp.logical_and(level >= k, position + step < slabs), 1, 0)
        partners += jnp.where(jnp.logical_and(level >= k, position >= step), 1, 0)
    pl.semaphore_wait(barrier, partners)

    def bond_copy():
        return remote(
            bond_out.at[core], bond_in.at[core], send_sem.at[0], bond_sem.at[0], position + 1, core
        )

    pl.when(sends_bond)(lambda: bond_copy().start())

    @pl.when(shallow)
    def _():
        arrival(bond_in.at[core], bond_sem.at[0]).wait_recv()
        join(bond_in.at[core], 0).start()
        own_bond = unpack(both_halves(bond_out))

        @pl.when(position < slabs - 1)
        def _():
            links[1] = own_bond

        @pl.when(position == slabs - 1)
        def _():
            for h in range(2):
                for plane in range(2):
                    first = plane * size + h * half
                    ground[h, plane] += own_bond[:, first : first + half]
            links[1] = jnp.zeros((size, 2 * size), F32)

        join(bond_in.at[twin], 0).wait_recv()
        links[0] = unpack(both_halves(bond_in))

    def add_terms(k, side):
        arrival(terms_in.at[k, side], terms_sem.at[k, side]).wait_recv()
        ground[core] += terms_in[k, side]

    def add_waves(k, side):
        arrival(waves_in.at[k, side], waves_sem.at[k, side]).wait_recv()
        waves[...] += waves_in[k, side, 0:size]
        flag[...] = jnp.maximum(flag[...], waves_in[k, side, size : size + 8])

    def add_waves_level(k):
        pl.when(not_root)(functools.partial(add_waves, k, 0))
        add_waves(k, 1)

    @pl.loop(0, jnp.maximum(level - 1, 0))
    def _(k):
        pl.when(not_root)(functools.partial(add_terms, k, 0))
        add_terms(k, 1)

    pl.when(inner)(lambda: join(ground.at[core], 5).start())

    def link_arrival(side):
        arrival(link_in.at[side, core], link_sem.at[side]).wait_recv()
        join(link_in.at[side, core], 6 + side).start()

    def link_whole(side):
        join(link_in.at[side, twin], 6 + side).wait_recv()
        links[side] = adjoint_of(whole(link_in.at[side]))

    pl.when(deep_left)(functools.partial(link_arrival, 0))
    pl.when(deep)(functools.partial(link_arrival, 1))
    pl.when(deep_left)(functools.partial(link_whole, 0))
    pl.when(deep)(functools.partial(link_whole, 1))

    @pl.loop(0, jnp.maximum(level - 2, 0))
    def _(k):
        add_waves_level(k)

    @pl.when(jnp.logical_not(not_root))
    def _():
        links[0] = jnp.zeros((size, 2 * size), F32)

    pl.when(inner)(lambda: join(ground.at[twin], 5).wait_recv())
    matrix[...] = whole(ground) + links[0] + links[1]

    def corner_arrival(side):
        arrival(corner_in.at[side, core], corner_sem.at[side]).wait_recv()
        join(corner_in.at[side, core], 1 + side).start()

    def corner_whole(side):
        join(corner_in.at[side, twin], 1 + side).wait_recv()
        term = unpack(both_halves(corner_in.at[side]))
        matrix[...] -= term
        links[side] -= term

    pl.when(inner_left)(functools.partial(corner_arrival, 0))
    pl.when(inner)(functools.partial(corner_arrival, 1))
    pl.when(inner_left)(functools.partial(corner_whole, 0))
    pl.when(inner)(functools.partial(corner_whole, 1))

    wide_row = lax.broadcasted_iota(jnp.int32, (size, 2 * size), 0)
    wide_column = lax.broadcasted_iota(jnp.int32, (size, 2 * size), 1)
    unit = jnp.where(wide_row == wide_column, 1.0, 0.0).astype(F32)
    mean = jnp.sum(matrix[...] * unit, keepdims=True) / size
    scale = 1.0 / mean
    scaled = matrix[...] * scale
    power = unit - scaled
    inverse = unit + power
    power = power.astype(BF16)
    power = dot(power, expand(power)).astype(BF16)
    for k in range(3):
        both = dot(jnp.concatenate([inverse.astype(BF16), power], 0), expand(power))
        inverse = inverse + both[:size]
        power = both[size:].astype(BF16)
    inverse = inverse + dot(inverse.astype(BF16), expand(power))
    inverse_pair = split(inverse)
    residual = unit - dot3(split(scaled), pair_map(expand, inverse_pair))
    inverse = inverse + dot3(inverse_pair, pair_map(expand, split(residual)))
    squared = jnp.sum(residual * residual, keepdims=True)
    bad = jnp.where(squared < RESIDUAL_LIMIT, 0.0, 1.0)
    flag[...] = jnp.maximum(flag[...], jnp.broadcast_to(bad, (8, 128)))
    solver = split(inverse * scale)

    def ground_arrival(side):
        arrival(ground_in.at[side, core], ground_sem.at[side]).wait_recv()
        join(ground_in.at[side, core], 3 + side).start()

    def ground_whole(side):
        join(ground_in.at[side, twin], 3 + side).wait_recv()
        links[side] -= whole(ground_in.at[side])
        ground[core] += ground_in[side, core]

    pl.when(inner_left)(functools.partial(ground_arrival, 0))
    pl.when(inner_left)(functools.partial(ground_arrival, 1))
    pl.when(inner)(lambda: join(ground.at[core], 5).wait_send())
    pl.when(inner_left)(functools.partial(ground_whole, 0))
    pl.when(inner_left)(functools.partial(ground_whole, 1))

    @pl.when(jnp.logical_not(has_right))
    def _():
        links[1] = jnp.zeros((size, 2 * size), F32)
        wave_in[1] = jnp.zeros(wave_in.shape[1:], F32)

    corner_copy = remote(
        corner_out.at[core],
        corner_in.at[far, core],
        send_sem.at[2],
        corner_sem.at[far],
        near_target,
        core,
    )
    ground_copy = remote(
        ground_out, ground_in.at[far, core], send_sem.at[3], ground_sem.at[far], near_target, core
    )
    waves_copy = remote(
        waves_out,
        waves_in.at[level, far],
        send_sem.at[4],
        waves_sem.at[level, far],
        near_target,
        core,
    )
    far_waves_copy = remote(
        far_waves_out,
        waves_in.at[level, near],
        send_sem.at[7],
        waves_sem.at[level, near],
        far_target,
        core,
    )
    far_copy = remote(
        far_out, terms_in.at[level, near], send_sem.at[5], terms_sem.at[level, near], far_target, core
    )
    link_copy = remote(
        link_out, link_in.at[near, core], send_sem.at[6], link_sem.at[near], far_target, core
    )

    def own_half(ref):
        return jnp.concatenate([ref[:, own_real], ref[:, own_imag]], 1)

    def turn_waves(value):
        swapped = jnp.where(
            lane % part_width < part_cols,
            -pltpu.roll(value, 128 - part_cols, 1),
            pltpu.roll(value, part_cols, 1),
        )
        return jnp.concatenate([value, swapped], 0)

    def expand_waves(value):
        high, low = split(value)
        high_wide, low_wide = high.astype(F32), low.astype(F32)
        return turn_waves(high_wide).astype(BF16), turn_waves(low_wide).astype(BF16)

    def pack_part(value):
        packed_part = value[0:part_rows]
        for q in range(1, PARTS):
            shifted = pltpu.roll(value[q * part_rows : (q + 1) * part_rows], q * part_width, 1)
            packed_part = jnp.where(lane >= q * part_width, shifted, packed_part)
        return packed_part

    def unpack_part(value):
        pieces = [value]
        for q in range(1, PARTS):
            pieces.append(pltpu.roll(value, 128 - q * part_width, 1))
        return jnp.concatenate(pieces, 0)

    def solve_waves():
        @pl.loop(jnp.maximum(level - 2, 0), level)
        def _(k):
            add_waves_level(k)

        solved = dot3(solver, expand_waves(waves[...]))
        waves[...] = solved
        return expand_waves(solved)

    @pl.when(jnp.logical_not(not_root))
    def _():
        solve_waves()

    @pl.when(not_root)
    def _():
        near_adjoint = adjoint_of(links[near])
        near_left = split(near_adjoint)
        sources = jnp.concatenate(
            [links[near, :, own_real], ground[core, 0], links[near, :, own_imag], ground[core, 1]], 1
        )
        solved = dot3(solver, pair_map(expand, split(sources)))
        both_terms = dot3(near_left, pair_map(expand, split(solved)))
        corner_out[core] = jnp.where(
            row >= column, both_terms[:, :half], both_terms[:, size : size + half]
        )
        corner_copy.start()
        pl.when(sends_link)(lambda: join(corner_out.at[core], 8).start())

        ground_out[0] = both_terms[:, half:size]
        ground_out[1] = both_terms[:, size + half :]
        pl.when(sends_ground)(lambda: ground_copy.start())

        @pl.when(sends_link)
        def _():
            join(corner_out.at[twin], 8).wait_recv()
            spare[...] = near_adjoint - unpack(both_halves(corner_out))
            link_out[0] = spare[:, own_real] - ground_out[0]
            link_out[1] = spare[:, own_imag] - ground_out[1]
            link_copy.start()

        solved_ground = pair_map(
            expand,
            split(jnp.concatenate([solved[:, half:size], solved[:, size + half :]], 1)),
        )
        far_left = split(adjoint_of(links[far]))

        @pl.when(has_right)
        def _():
            product = dot3(far_left, solved_ground)
            far_out[0] = product[:, :half]
            far_out[1] = product[:, half:]
            far_copy.start()

        solved_waves = solve_waves()
        waves_out[0:size] = dot3(near_left, solved_waves)
        waves_out[size : size + 8] = flag[...]
        waves_copy.start()

        @pl.when(has_right)
        def _():
            far_waves_out[0:size] = dot3(far_left, solved_waves)
            far_waves_out[size : size + 8] = flag[...]
            far_waves_copy.start()

        for side in range(2):
            spike = split(dot3(solver, pair_map(expand, split(links[side]))))
            for part in range(2):
                back[part, :, side * 2 * size : (side + 1) * 2 * size] = spike[part]

    def wave_sends(k, step, p):
        to_right = remote(
            wave_out.at[p], wave_in.at[0, p], wave_send_sem.at[0, p], wave_sem.at[0, p], position + step, core
        )
        to_left = remote(
            wave_out.at[p], wave_in.at[1, p], wave_send_sem.at[1, p], wave_sem.at[1, p], position - step, core
        )
        return to_right, to_left

    def start_waves(k, step, p):
        to_right, to_left = wave_sends(k, step, p)
        to_right.start()
        pl.when(not_root)(lambda: to_left.start())

    def finish_waves(k, step, p):
        to_right, to_left = wave_sends(k, step, p)
        to_right.wait_send()
        pl.when(not_root)(lambda: to_left.wait_send())

    first_step = jnp.where(inner, stride // 2, 1)
    rows_flag = pl.ds(part_rows, 8)
    for p in range(PARTS):
        own = pltpu.roll(waves[...], 128 - p * part_width, 1) if p else waves[...]
        wave_out[p, 0:part_rows] = pack_part(own)

        @pl.when(not_root)
        def _():
            arrival(wave_in.at[0, p], wave_sem.at[0, p]).wait_recv()
            pl.when(has_right)(lambda: arrival(wave_in.at[1, p], wave_sem.at[1, p]).wait_recv())
            sides = [expand_waves(unpack_part(wave_in[side, p, 0:part_rows])) for side in range(2)]
            pair = [jnp.concatenate([sides[0][e], sides[1][e]], 0) for e in range(2)]
            total = dot3((back[0], back[1]), pair)
            wave_out[p, 0:part_rows] += pack_part(total)
            if p == 0:
                flag[...] = jnp.maximum(flag[...], wave_in[0, 0, rows_flag])

        wave_out[p, rows_flag] = flag[...]
        pl.when(inner)(functools.partial(start_waves, level - 1, first_step, p))

    @pl.when(inner)
    def _():
        for p in range(PARTS):
            finish_waves(level - 1, first_step, p)

    @pl.loop(1, level)
    def _(down):
        k = level - 1 - down
        step = jnp.int32(1)
        for m in range(1, levels):
            step = step + jnp.where(k >= m, 1 << (m - 1), 0)
        for p in range(PARTS):
            start_waves(k, step, p)
        for p in range(PARTS):
            finish_waves(k, step, p)

    turned_waves = jnp.concatenate(
        [unpack_part(wave_out[p, 0:part_rows])[:, :part_width] for p in range(PARTS)], 1
    ).T
    for p in range(PARTS):
        for plane in range(2):
            first = p * part_width + plane * part_cols
            out_ref[0, plane, p * part_cols : (p + 1) * part_cols] = turned_waves[first : first + part_cols]
    flag_ref[...] = flag[...]

    pl.when(sends_bond)(lambda: bond_copy().wait_send())
    pl.when(shallow)(lambda: join(bond_in.at[core], 0).wait_send())
    for side in range(2):
        pl.when(deep_left if side == 0 else deep)(
            lambda: join(link_in.at[side, core], 6 + side).wait_send()
        )
        pl.when(inner_left if side == 0 else inner)(
            lambda: join(corner_in.at[side, core], 1 + side).wait_send()
        )
        pl.when(inner_left)(lambda: join(ground_in.at[side, core], 3 + side).wait_send())

    @pl.when(not_root)
    def _():
        corner_copy.wait_send()
        pl.when(sends_ground)(lambda: ground_copy.wait_send())
        waves_copy.wait_send()

        @pl.when(has_right)
        def _():
            far_copy.wait_send()
            far_waves_copy.wait_send()

    @pl.when(sends_link)
    def _():
        join(corner_out.at[core], 8).wait_send()
        link_copy.wait_send()


def tree_path(slabs, bond_factor, tile_mask, potential, injection):
    size = bond_factor.shape[2]
    half = size // 2
    levels = slabs.bit_length() - 1
    vmem = pl.BlockSpec(memory_space=pltpu.VMEM)
    dma = pltpu.SemaphoreType.DMA
    turned = jnp.swapaxes(injection, 2, 3)
    amplitude, flag = pl.pallas_call(
        functools.partial(tree_kernel, slabs),
        out_shape=(
            jax.ShapeDtypeStruct(turned.shape, F32),
            jax.ShapeDtypeStruct((8, 128), F32),
        ),
        in_specs=[vmem, pl.BlockSpec(memory_space=pltpu.SMEM), vmem, vmem],
        out_specs=(vmem, vmem),
        scratch_shapes=[
            pltpu.VMEM((2, 2, size, half), F32),
            pltpu.VMEM((2, size, 2 * size), F32),
            pltpu.VMEM((size, 2 * size), F32),
            pltpu.VMEM((size, 2 * size), F32),
            pltpu.VMEM((size, 128), F32),
            pltpu.VMEM((8, 128), F32),
            pltpu.VMEM((2, size, half), F32),
            pltpu.VMEM((2, size, half), F32),
            pltpu.VMEM((2, size, half), F32),
            pltpu.VMEM((2, 2, size, half), F32),
            pltpu.VMEM((2, size, half), F32),
            pltpu.VMEM((2, 2, 2, size, half), F32),
            pltpu.VMEM((size + 8, 128), F32),
            pltpu.VMEM((size + 8, 128), F32),
            pltpu.VMEM((levels, 2, size + 8, 128), F32),
            pltpu.VMEM((2, size, half), F32),
            pltpu.VMEM((2, 2, 2, size, half), F32),
            pltpu.VMEM((2, size, half), F32),
            pltpu.VMEM((levels, 2, 2, size, half), F32),
            pltpu.VMEM((2, PARTS, size // PARTS + 8, 128), F32),
            pltpu.VMEM((PARTS, size // PARTS + 8, 128), F32),
            pltpu.VMEM((2, size, 4 * size), BF16),
            dma((8,)),
            dma((1,)),
            dma((2,)),
            dma((2,)),
            dma((levels, 2)),
            dma((2,)),
            dma((levels, 2)),
            dma((2, PARTS)),
            dma((2, PARTS)),
            dma((9,)),
            dma((9,)),
        ],
        compiler_params=pltpu.CompilerParams(
            collective_id=0, has_side_effects=True, vmem_limit_bytes=52 << 20
        ),
        name="tree_reduction",
    )(bond_factor, tile_mask, potential, turned)
    return jnp.swapaxes(amplitude, 2, 3), flag


def per_device(slabs, bond_factor, tile_mask, potential, injection):
    amplitude, flag = tree_path(slabs, bond_factor, tile_mask, potential, injection)

    def direct(state):
        return jnp.float32(0.0), direct_path(bond_factor, tile_mask, potential, injection)

    return lax.while_loop(lambda state: state[0] > 0.0, direct, (flag[0, 0], amplitude))[1]


def solution(mesh):
    in_specs = (
        P("slab", None, None, None),
        P("slab", None, None),
        P("slab", None),
        P("slab", None, None, "rhs"),
    )
    out_specs = P("slab", None, None, "rhs")
    return jax.shard_map(
        functools.partial(per_device, mesh.shape["slab"]),
        mesh=mesh,
        in_specs=in_specs,
        out_specs=out_specs,
        check_vma=False,
    )
```

```python
import functools

import jax
import jax.numpy as jnp
from jax import lax
from jax.experimental import pallas as pl
from jax.experimental.pallas import tpu as pltpu
from jax.sharding import PartitionSpec as P

PRECISE = lax.Precision.HIGHEST
MESH = pl.DeviceIdType.MESH
F32 = jnp.float32
BF16 = jnp.bfloat16
RESIDUAL_LIMIT = 4.0e-4
PARTS = 4


def passed_along(array, axis, by):
    length = lax.axis_size(axis)
    pairs = [(i, i + by) for i in range(length) if 0 <= i + by < length]
    return lax.ppermute(array, axis, pairs)


def matmul_exact(operand, other):
    return jnp.dot(operand, other, precision=PRECISE)


def transposed_product(operand, other):
    return lax.dot_general(operand, other, (((0,), (0,)), ((), ())), precision=PRECISE)


def complex_product(operand, other):
    real_part = matmul_exact(operand[0], other[0]) - matmul_exact(operand[1], other[1])
    imag_part = matmul_exact(operand[0], other[1]) + matmul_exact(operand[1], other[0])
    return jnp.stack([real_part, imag_part])


def adjoint_product(operand, other):
    real_part = transposed_product(operand[0], other[0]) + transposed_product(operand[1], other[1])
    imag_part = transposed_product(operand[0], other[1]) - transposed_product(operand[1], other[0])
    return jnp.stack([real_part, imag_part])


def adjoint(operand):
    return jnp.stack([operand[0].T, -operand[1].T])


def real_form(matrix):
    return jnp.block([[matrix[0], -matrix[1]], [matrix[1], matrix[0]]])


def solve_stacked(factor_low, stacked):
    forward_part = lax.linalg.triangular_solve(factor_low, stacked, left_side=True, lower=True)
    return lax.linalg.triangular_solve(
        factor_low, forward_part, left_side=True, lower=True, transpose_a=True
    )


def direct_path(bond_factor, tile_mask, potential, injection):
    orbitals = bond_factor.shape[2]
    tile_size = orbitals // tile_mask.shape[2]
    slab_total = lax.axis_size("slab")
    position = lax.axis_index("slab")
    core_total = lax.axis_size("rhs")
    core_index = lax.axis_index("rhs")
    half_cols = orbitals // core_total
    pattern = jnp.repeat(jnp.repeat(tile_mask[0], tile_size, 0), tile_size, 1).astype(
        bond_factor.dtype
    )
    factor = bond_factor[0] * pattern[None]
    bond_matrix = complex_product(factor, adjoint(factor))
    previous = passed_along(bond_matrix, "slab", 1)
    onsite = jnp.stack([jnp.diag(potential[0]), jnp.zeros((orbitals, orbitals), potential.dtype)])
    matrix = onsite + bond_matrix + previous
    coupling_up = jnp.where(position == slab_total - 1, jnp.zeros_like(bond_matrix), -bond_matrix)
    coupling_down = -previous
    sources = injection[0]

    def apply_inverse(block, right_side):
        factor_low = jnp.linalg.cholesky(real_form(block))
        stacked = jnp.concatenate([right_side[0], right_side[1]], 0)
        solved = solve_stacked(factor_low, stacked)
        return jnp.stack([solved[:orbitals], solved[orbitals:]])

    def own_columns(block):
        return lax.dynamic_slice_in_dim(block, core_index * half_cols, half_cols, 2)

    levels = slab_total.bit_length() - 1
    for rank_bit in range(levels):
        stride = 1 << rank_bit
        spikes = apply_inverse(
            matrix,
            jnp.concatenate([own_columns(coupling_up), own_columns(coupling_down), sources], 2),
        )
        spike_up = spikes[:, :, :half_cols]
        spike_down = spikes[:, :, half_cols : 2 * half_cols]
        spike_waves = spikes[:, :, 2 * half_cols :]
        toward_upper = adjoint_product(
            coupling_down, jnp.concatenate([spike_down, spike_up, spike_waves], 2)
        )
        from_upper = passed_along(toward_upper, "slab", -stride)
        cross_part = toward_upper[:, :, half_cols : 2 * half_cols]
        toward_lower = adjoint_product(coupling_up, jnp.concatenate([spike_up, spike_waves], 2))
        outgoing = jnp.concatenate(
            [toward_lower[:, :, :half_cols], cross_part, toward_lower[:, :, half_cols:]], 2
        )
        from_lower = passed_along(outgoing, "slab", stride)
        diag_change = from_upper[:, :, :half_cols] + from_lower[:, :, :half_cols]
        new_up = -from_upper[:, :, half_cols : 2 * half_cols]
        coupling_new = from_lower[:, :, half_cols : 2 * half_cols]
        sources = sources - from_upper[:, :, 2 * half_cols :] - from_lower[:, :, 2 * half_cols :]
        gathered = (
            lax.all_gather(diag_change, "rhs", axis=2, tiled=True),
            lax.all_gather(new_up, "rhs", axis=2, tiled=True),
            lax.all_gather(coupling_new, "rhs", axis=2, tiled=True),
        )
        matrix = matrix - gathered[0]
        coupling_up = gathered[1]
        coupling_down = -adjoint(gathered[2])
    amplitude = apply_inverse(matrix, sources)
    return amplitude[None]


def split(value):
    high = value.astype(BF16)
    low = (value - high.astype(F32)).astype(BF16)
    return high, low


def dot(left, right):
    return jnp.dot(left, right, preferred_element_type=F32)


def dot3(left, right):
    high = dot(left[0], right[0])
    return high + (dot(left[0], right[1]) + dot(left[1], right[0]))


def pair_map(function, pair):
    return function(pair[0]), function(pair[1])


def tree_kernel(
    slabs,
    factor_ref,
    mask_ref,
    potential_ref,
    injection_ref,
    out_ref,
    flag_ref,
    ground,
    links,
    matrix,
    spare,
    waves,
    flag,
    bond_out,
    bond_in,
    corner_out,
    corner_in,
    ground_out,
    ground_in,
    waves_out,
    far_waves_out,
    waves_in,
    link_out,
    link_in,
    far_out,
    terms_in,
    wave_in,
    wave_out,
    back,
    send_sem,
    bond_sem,
    corner_sem,
    ground_sem,
    waves_sem,
    link_sem,
    terms_sem,
    wave_sem,
    wave_send_sem,
    join_send_sem,
    join_sem,
):
    size = factor_ref.shape[2]
    half = size // 2
    cols = injection_ref.shape[2]
    part_cols = cols // PARTS
    part_width = 2 * part_cols
    part_rows = size // PARTS
    tile = size // mask_ref.shape[2]
    position = lax.axis_index("slab")
    core = lax.axis_index("rhs")
    twin = 1 - core
    levels = slabs.bit_length() - 1

    level = jnp.int32(0)
    stride = jnp.int32(1)
    for k in range(1, levels + 1):
        even = jnp.where(position % (1 << k) == 0, 1, 0)
        level = level + even
        stride = stride + even * (1 << (k - 1))
    not_root = position > 0
    inner = level > 0
    inner_left = jnp.logical_and(inner, not_root)
    deep = level > 1
    deep_left = jnp.logical_and(deep, not_root)
    shallow = position % 4 != 0
    has_right = jnp.logical_and(not_root, position + stride < slabs)
    near_is_right = jnp.logical_and(has_right, (position // stride) % 4 == 1)
    near = jnp.where(near_is_right, 1, 0)
    far = 1 - near
    near_target = jnp.where(near_is_right, position + stride, position - stride)
    far_target = jnp.where(near_is_right, position - stride, position + stride)
    near_is_root = near_target == 0
    sends_ground = jnp.logical_and(not_root, jnp.logical_not(near_is_root))
    sends_link = jnp.logical_and(
        has_right, jnp.logical_or((far_target // stride) % 8 == 4, jnp.logical_and(far_target == 0, stride * 4 == slabs))
    )
    sends_bond = (position + 1) % 4 != 0

    def remote(source, target, sent, received, slab_to, core_to):
        return pltpu.make_async_remote_copy(
            src_ref=source,
            dst_ref=target,
            send_sem=sent,
            recv_sem=received,
            device_id=(slab_to, core_to),
            device_id_type=MESH,
        )

    def arrival(block, received):
        return remote(block, block, send_sem.at[1], received, position, twin)

    def join(block, which):
        return remote(block, block, join_send_sem.at[which], join_sem.at[which], position, twin)

    row = lax.broadcasted_iota(jnp.int32, (size, half), 0)
    lane_half = lax.broadcasted_iota(jnp.int32, (size, half), 1)
    column = lane_half + core * half
    square_row = lax.broadcasted_iota(jnp.int32, (size, size), 0)
    square_column = lax.broadcasted_iota(jnp.int32, (size, size), 1)
    own_real = pl.ds(pl.multiple_of(core * half, half), half)
    own_imag = pl.ds(pl.multiple_of(core * half + size, half), half)

    for h in range(2):
        energies = jnp.broadcast_to(potential_ref[:, h * half : (h + 1) * half], (size, half))
        ground[h, 0] = jnp.where(row == lane_half + h * half, energies, 0.0)
        ground[h, 1] = jnp.zeros((size, half), F32)

    barrier = pltpu.get_barrier_semaphore()

    def greet(slab_to, core_to):
        pl.semaphore_signal(barrier, inc=1, device_id=(slab_to, core_to), device_id_type=MESH)

    greet(position, twin)
    for k in range(levels):
        step = 1 << k
        pl.when(jnp.logical_and(level >= k, position + step < slabs))(
            functools.partial(greet, position + step, core)
        )
        pl.when(jnp.logical_and(level >= k, position >= step))(
            functools.partial(greet, position - step, core)
        )

    def turn(value):
        width = value.shape[1] // 2
        return jnp.concatenate([-value[:, width:], value[:, :width]], 1)

    def expand(value):
        return jnp.concatenate([value, turn(value)], 0)

    def adjoint_of(value):
        return jnp.concatenate([value[:, :size].T, -value[:, size:].T], 1)

    def unpack(square):
        turned = square.T
        real = jnp.where(square_row >= square_column, square, turned)
        below = jnp.where(square_row > square_column, -turned, 0.0)
        imag = jnp.where(square_row < square_column, square, below)
        return jnp.concatenate([real, imag], 1)

    def both_halves(block):
        return jnp.concatenate([block[0], block[1]], 1)

    def whole(block):
        return jnp.concatenate([block[0, 0], block[1, 0], block[0, 1], block[1, 1]], 1)

    lane = lax.broadcasted_iota(jnp.int32, (1, 128), 1)
    masked = []
    for plane in range(2):
        rows = []
        for r in range(size // tile):
            blocks = []
            for k in range(size // 128):
                keep = mask_ref[0, r, k * 128 // tile].astype(F32)
                for t in range(1, 128 // tile):
                    other = mask_ref[0, r, k * 128 // tile + t].astype(F32)
                    keep = jnp.where(lane >= t * tile, other, keep)
                piece = factor_ref[0, plane, r * tile : (r + 1) * tile, k * 128 : (k + 1) * 128]
                blocks.append(piece * keep)
            rows.append(jnp.concatenate(blocks, 1))
        masked.append(jnp.concatenate(rows, 0))
    factor = jnp.concatenate(masked, 1)
    bond = dot3(split(factor), pair_map(expand, split(adjoint_of(factor))))
    packed = jnp.where(square_row >= square_column, bond[:, :size], bond[:, size:])
    bond_out[0] = packed[:, :half]
    bond_out[1] = packed[:, half:]

    waves[...] = jnp.concatenate(
        [
            injection_ref[0, plane, p * part_cols : (p + 1) * part_cols]
            for p in range(PARTS)
            for plane in range(2)
        ],
        0,
    ).T
    flag[...] = jnp.zeros_like(flag)

    partners = jnp.int32(1)
    for k in range(levels):
        step = 1 << k
        partners += jnp.where(jnp.logical_and(level >= k, position + step < slabs), 1, 0)
        partners += jnp.where(jnp.logical_and(level >= k, position >= step), 1, 0)
    pl.semaphore_wait(barrier, partners)

    def bond_copy():
        return remote(
            bond_out.at[core], bond_in.at[core], send_sem.at[0], bond_sem.at[0], position + 1, core
        )

    pl.when(sends_bond)(lambda: bond_copy().start())

    @pl.when(shallow)
    def _():
        arrival(bond_in.at[core], bond_sem.at[0]).wait_recv()
        join(bond_in.at[core], 0).start()
        own_bond = unpack(both_halves(bond_out))

        @pl.when(position < slabs - 1)
        def _():
            links[1] = own_bond

        @pl.when(position == slabs - 1)
        def _():
            for h in range(2):
                for plane in range(2):
                    first = plane * size + h * half
                    ground[h, plane] += own_bond[:, first : first + half]
            links[1] = jnp.zeros((size, 2 * size), F32)

        join(bond_in.at[twin], 0).wait_recv()
        links[0] = unpack(both_halves(bond_in))

    def add_terms(k, side):
        arrival(terms_in.at[k, side], terms_sem.at[k, side]).wait_recv()
        ground[core] += terms_in[k, side]

    def add_waves(k, side):
        arrival(waves_in.at[k, side], waves_sem.at[k, side]).wait_recv()
        waves[...] += waves_in[k, side, 0:size]
        flag[...] = jnp.maximum(flag[...], waves_in[k, side, size : size + 8])

    def add_waves_level(k):
        pl.when(not_root)(functools.partial(add_waves, k, 0))
        add_waves(k, 1)

    @pl.loop(0, jnp.maximum(level - 1, 0))
    def _(k):
        pl.when(not_root)(functools.partial(add_terms, k, 0))
        add_terms(k, 1)

    pl.when(inner)(lambda: join(ground.at[core], 5).start())

    def link_arrival(side):
        arrival(link_in.at[side, core], link_sem.at[side]).wait_recv()
        join(link_in.at[side, core], 6 + side).start()

    def link_whole(side):
        join(link_in.at[side, twin], 6 + side).wait_recv()
        links[side] = adjoint_of(whole(link_in.at[side]))

    pl.when(deep_left)(functools.partial(link_arrival, 0))
    pl.when(deep)(functools.partial(link_arrival, 1))
    pl.when(deep_left)(functools.partial(link_whole, 0))
    pl.when(deep)(functools.partial(link_whole, 1))

    @pl.loop(0, jnp.maximum(level - 2, 0))
    def _(k):
        add_waves_level(k)

    @pl.when(jnp.logical_not(not_root))
    def _():
        links[0] = jnp.zeros((size, 2 * size), F32)

    pl.when(inner)(lambda: join(ground.at[twin], 5).wait_recv())
    matrix[...] = whole(ground) + links[0] + links[1]

    def corner_arrival(side):
        arrival(corner_in.at[side, core], corner_sem.at[side]).wait_recv()
        join(corner_in.at[side, core], 1 + side).start()

    def corner_whole(side):
        join(corner_in.at[side, twin], 1 + side).wait_recv()
        term = unpack(both_halves(corner_in.at[side]))
        matrix[...] -= term
        links[side] -= term

    pl.when(inner_left)(functools.partial(corner_arrival, 0))
    pl.when(inner)(functools.partial(corner_arrival, 1))
    pl.when(inner_left)(functools.partial(corner_whole, 0))
    pl.when(inner)(functools.partial(corner_whole, 1))

    wide_row = lax.broadcasted_iota(jnp.int32, (size, 2 * size), 0)
    wide_column = lax.broadcasted_iota(jnp.int32, (size, 2 * size), 1)
    unit = jnp.where(wide_row == wide_column, 1.0, 0.0).astype(F32)
    mean = jnp.sum(matrix[...] * unit, keepdims=True) / size
    scale = 1.0 / mean
    scaled = matrix[...] * scale
    power = unit - scaled
    inverse = unit + power
    power = power.astype(BF16)
    power = dot(power, expand(power)).astype(BF16)
    for k in range(3):
        both = dot(jnp.concatenate([inverse.astype(BF16), power], 0), expand(power))
        inverse = inverse + both[:size]
        power = both[size:].astype(BF16)
    inverse = inverse + dot(inverse.astype(BF16), expand(power))
    inverse_pair = split(inverse)
    residual = unit - dot3(split(scaled), pair_map(expand, inverse_pair))
    inverse = inverse + dot3(inverse_pair, pair_map(expand, split(residual)))
    squared = jnp.sum(residual * residual, keepdims=True)
    bad = jnp.where(squared < RESIDUAL_LIMIT, 0.0, 1.0)
    flag[...] = jnp.maximum(flag[...], jnp.broadcast_to(bad, (8, 128)))
    solver = split(inverse * scale)

    def ground_arrival(side):
        arrival(ground_in.at[side, core], ground_sem.at[side]).wait_recv()
        join(ground_in.at[side, core], 3 + side).start()

    def ground_whole(side):
        join(ground_in.at[side, twin], 3 + side).wait_recv()
        links[side] -= whole(ground_in.at[side])
        ground[core] += ground_in[side, core]

    pl.when(inner_left)(functools.partial(ground_arrival, 0))
    pl.when(inner_left)(functools.partial(ground_arrival, 1))
    pl.when(inner)(lambda: join(ground.at[core], 5).wait_send())
    pl.when(inner_left)(functools.partial(ground_whole, 0))
    pl.when(inner_left)(functools.partial(ground_whole, 1))

    @pl.when(jnp.logical_not(has_right))
    def _():
        links[1] = jnp.zeros((size, 2 * size), F32)
        wave_in[1] = jnp.zeros(wave_in.shape[1:], F32)

    corner_copy = remote(
        corner_out.at[core],
        corner_in.at[far, core],
        send_sem.at[2],
        corner_sem.at[far],
        near_target,
        core,
    )
    ground_copy = remote(
        ground_out, ground_in.at[far, core], send_sem.at[3], ground_sem.at[far], near_target, core
    )
    waves_copy = remote(
        waves_out,
        waves_in.at[level, far],
        send_sem.at[4],
        waves_sem.at[level, far],
        near_target,
        core,
    )
    far_waves_copy = remote(
        far_waves_out,
        waves_in.at[level, near],
        send_sem.at[7],
        waves_sem.at[level, near],
        far_target,
        core,
    )
    far_copy = remote(
        far_out, terms_in.at[level, near], send_sem.at[5], terms_sem.at[level, near], far_target, core
    )
    link_copy = remote(
        link_out, link_in.at[near, core], send_sem.at[6], link_sem.at[near], far_target, core
    )

    def own_half(ref):
        return jnp.concatenate([ref[:, own_real], ref[:, own_imag]], 1)

    def turn_waves(value):
        swapped = jnp.where(
            lane % part_width < part_cols,
            -pltpu.roll(value, 128 - part_cols, 1),
            pltpu.roll(value, part_cols, 1),
        )
        return jnp.concatenate([value, swapped], 0)

    def expand_waves(value):
        high, low = split(value)
        high_wide, low_wide = high.astype(F32), low.astype(F32)
        return turn_waves(high_wide).astype(BF16), turn_waves(low_wide).astype(BF16)

    def pack_part(value):
        packed_part = value[0:part_rows]
        for q in range(1, PARTS):
            shifted = pltpu.roll(value[q * part_rows : (q + 1) * part_rows], q * part_width, 1)
            packed_part = jnp.where(lane >= q * part_width, shifted, packed_part)
        return packed_part

    def unpack_part(value):
        pieces = [value]
        for q in range(1, PARTS):
            pieces.append(pltpu.roll(value, 128 - q * part_width, 1))
        return jnp.concatenate(pieces, 0)

    def solve_waves():
        @pl.loop(jnp.maximum(level - 2, 0), level)
        def _(k):
            add_waves_level(k)

        solved = dot3(solver, expand_waves(waves[...]))
        waves[...] = solved
        return expand_waves(solved)

    @pl.when(jnp.logical_not(not_root))
    def _():
        solve_waves()

    @pl.when(not_root)
    def _():
        near_adjoint = adjoint_of(links[near])
        near_left = split(near_adjoint)
        solved = dot3(solver, pair_map(expand, split(own_half(links.at[near]))))
        solved_near = pair_map(expand, split(solved))
        product = dot3(near_left, solved_near)
        corner_out[core] = jnp.where(row >= column, product[:, :half], product[:, half:])
        corner_copy.start()
        pl.when(sends_link)(lambda: join(corner_out.at[core], 8).start())

        own_ground = jnp.concatenate([ground[core, 0], ground[core, 1]], 1)
        solved = dot3(solver, pair_map(expand, split(own_ground)))
        solved_ground = pair_map(expand, split(solved))

        product = dot3(near_left, solved_ground)
        ground_out[0] = product[:, :half]
        ground_out[1] = product[:, half:]
        pl.when(sends_ground)(lambda: ground_copy.start())

        @pl.when(sends_link)
        def _():
            join(corner_out.at[twin], 8).wait_recv()
            spare[...] = near_adjoint - unpack(both_halves(corner_out))
            link_out[0] = spare[:, own_real] - ground_out[0]
            link_out[1] = spare[:, own_imag] - ground_out[1]
            link_copy.start()

        far_left = split(adjoint_of(links[far]))

        @pl.when(has_right)
        def _():
            product = dot3(far_left, solved_ground)
            far_out[0] = product[:, :half]
            far_out[1] = product[:, half:]
            far_copy.start()

        solved_waves = solve_waves()
        waves_out[0:size] = dot3(near_left, solved_waves)
        waves_out[size : size + 8] = flag[...]
        waves_copy.start()

        @pl.when(has_right)
        def _():
            far_waves_out[0:size] = dot3(far_left, solved_waves)
            far_waves_out[size : size + 8] = flag[...]
            far_waves_copy.start()

        for side in range(2):
            spike = split(dot3(solver, pair_map(expand, split(links[side]))))
            for part in range(2):
                back[part, :, side * 2 * size : (side + 1) * 2 * size] = spike[part]

    def wave_sends(k, step, p):
        to_right = remote(
            wave_out.at[p], wave_in.at[0, p], wave_send_sem.at[0, p], wave_sem.at[0, p], position + step, core
        )
        to_left = remote(
            wave_out.at[p], wave_in.at[1, p], wave_send_sem.at[1, p], wave_sem.at[1, p], position - step, core
        )
        return to_right, to_left

    def start_waves(k, step, p):
        to_right, to_left = wave_sends(k, step, p)
        to_right.start()
        pl.when(not_root)(lambda: to_left.start())

    def finish_waves(k, step, p):
        to_right, to_left = wave_sends(k, step, p)
        to_right.wait_send()
        pl.when(not_root)(lambda: to_left.wait_send())

    first_step = jnp.where(inner, stride // 2, 1)
    rows_flag = pl.ds(part_rows, 8)
    for p in range(PARTS):
        own = pltpu.roll(waves[...], 128 - p * part_width, 1) if p else waves[...]
        wave_out[p, 0:part_rows] = pack_part(own)

        @pl.when(not_root)
        def _():
            arrival(wave_in.at[0, p], wave_sem.at[0, p]).wait_recv()
            pl.when(has_right)(lambda: arrival(wave_in.at[1, p], wave_sem.at[1, p]).wait_recv())
            sides = [expand_waves(unpack_part(wave_in[side, p, 0:part_rows])) for side in range(2)]
            pair = [jnp.concatenate([sides[0][e], sides[1][e]], 0) for e in range(2)]
            total = dot3((back[0], back[1]), pair)
            wave_out[p, 0:part_rows] += pack_part(total)
            if p == 0:
                flag[...] = jnp.maximum(flag[...], wave_in[0, 0, rows_flag])

        wave_out[p, rows_flag] = flag[...]
        pl.when(inner)(functools.partial(start_waves, level - 1, first_step, p))

    @pl.when(inner)
    def _():
        for p in range(PARTS):
            finish_waves(level - 1, first_step, p)

    @pl.loop(1, level)
    def _(down):
        k = level - 1 - down
        step = jnp.int32(1)
        for m in range(1, levels):
            step = step + jnp.where(k >= m, 1 << (m - 1), 0)
        for p in range(PARTS):
            start_waves(k, step, p)
        for p in range(PARTS):
            finish_waves(k, step, p)

    turned_waves = jnp.concatenate(
        [unpack_part(wave_out[p, 0:part_rows])[:, :part_width] for p in range(PARTS)], 1
    ).T
    for p in range(PARTS):
        for plane in range(2):
            first = p * part_width + plane * part_cols
            out_ref[0, plane, p * part_cols : (p + 1) * part_cols] = turned_waves[first : first + part_cols]
    flag_ref[...] = flag[0:1, 0:1]

    pl.when(sends_bond)(lambda: bond_copy().wait_send())
    pl.when(shallow)(lambda: join(bond_in.at[core], 0).wait_send())
    for side in range(2):
        pl.when(deep_left if side == 0 else deep)(
            lambda: join(link_in.at[side, core], 6 + side).wait_send()
        )
        pl.when(inner_left if side == 0 else inner)(
            lambda: join(corner_in.at[side, core], 1 + side).wait_send()
        )
        pl.when(inner_left)(lambda: join(ground_in.at[side, core], 3 + side).wait_send())

    @pl.when(not_root)
    def _():
        corner_copy.wait_send()
        pl.when(sends_ground)(lambda: ground_copy.wait_send())
        waves_copy.wait_send()

        @pl.when(has_right)
        def _():
            far_copy.wait_send()
            far_waves_copy.wait_send()

    @pl.when(sends_link)
    def _():
        join(corner_out.at[core], 8).wait_send()
        link_copy.wait_send()


def tree_path(slabs, bond_factor, tile_mask, potential, injection):
    size = bond_factor.shape[2]
    half = size // 2
    levels = slabs.bit_length() - 1
    vmem = pl.BlockSpec(memory_space=pltpu.VMEM)
    dma = pltpu.SemaphoreType.DMA
    turned = jnp.swapaxes(injection, 2, 3)
    amplitude, flag = pl.pallas_call(
        functools.partial(tree_kernel, slabs),
        out_shape=(
            jax.ShapeDtypeStruct(turned.shape, F32),
            jax.ShapeDtypeStruct((1, 1), F32),
        ),
        in_specs=[vmem, pl.BlockSpec(memory_space=pltpu.SMEM), vmem, vmem],
        out_specs=(vmem, vmem),
        scratch_shapes=[
            pltpu.VMEM((2, 2, size, half), F32),
            pltpu.VMEM((2, size, 2 * size), F32),
            pltpu.VMEM((size, 2 * size), F32),
            pltpu.VMEM((size, 2 * size), F32),
            pltpu.VMEM((size, 128), F32),
            pltpu.VMEM((8, 128), F32),
            pltpu.VMEM((2, size, half), F32),
            pltpu.VMEM((2, size, half), F32),
            pltpu.VMEM((2, size, half), F32),
            pltpu.VMEM((2, 2, size, half), F32),
            pltpu.VMEM((2, size, half), F32),
            pltpu.VMEM((2, 2, 2, size, half), F32),
            pltpu.VMEM((size + 8, 128), F32),
            pltpu.VMEM((size + 8, 128), F32),
            pltpu.VMEM((levels, 2, size + 8, 128), F32),
            pltpu.VMEM((2, size, half), F32),
            pltpu.VMEM((2, 2, 2, size, half), F32),
            pltpu.VMEM((2, size, half), F32),
            pltpu.VMEM((levels, 2, 2, size, half), F32),
            pltpu.VMEM((2, PARTS, size // PARTS + 8, 128), F32),
            pltpu.VMEM((PARTS, size // PARTS + 8, 128), F32),
            pltpu.VMEM((2, size, 4 * size), BF16),
            dma((8,)),
            dma((1,)),
            dma((2,)),
            dma((2,)),
            dma((levels, 2)),
            dma((2,)),
            dma((levels, 2)),
            dma((2, PARTS)),
            dma((2, PARTS)),
            dma((9,)),
            dma((9,)),
        ],
        compiler_params=pltpu.CompilerParams(
            collective_id=0, has_side_effects=True, vmem_limit_bytes=52 << 20
        ),
        name="tree_reduction",
    )(bond_factor, tile_mask, potential, turned)
    return jnp.swapaxes(amplitude, 2, 3), flag


def per_device(slabs, bond_factor, tile_mask, potential, injection):
    amplitude, flag = tree_path(slabs, bond_factor, tile_mask, potential, injection)
    return lax.cond(
        flag[0, 0] == 0.0,
        lambda *operands: amplitude,
        direct_path,
        bond_factor,
        tile_mask,
        potential,
        injection,
    )


def solution(mesh):
    in_specs = (
        P("slab", None, None, None),
        P("slab", None, None),
        P("slab", None),
        P("slab", None, None, "rhs"),
    )
    out_specs = P("slab", None, None, "rhs")
    return jax.shard_map(
        functools.partial(per_device, mesh.shape["slab"]),
        mesh=mesh,
        in_specs=in_specs,
        out_specs=out_specs,
        check_vma=False,
    )
```

```python
import functools

import jax
import jax.numpy as jnp
from jax import lax
from jax.experimental import pallas as pl
from jax.experimental.pallas import tpu as pltpu
from jax.sharding import PartitionSpec as P

PRECISE = lax.Precision.HIGHEST
MESH = pl.DeviceIdType.MESH
F32 = jnp.float32
BF16 = jnp.bfloat16
RESIDUAL_LIMIT = 4.0e-4
PARTS = 4


def passed_along(array, axis, by):
    length = lax.axis_size(axis)
    pairs = [(i, i + by) for i in range(length) if 0 <= i + by < length]
    return lax.ppermute(array, axis, pairs)


def matmul_exact(operand, other):
    return jnp.dot(operand, other, precision=PRECISE)


def transposed_product(operand, other):
    return lax.dot_general(operand, other, (((0,), (0,)), ((), ())), precision=PRECISE)


def complex_product(operand, other):
    real_part = matmul_exact(operand[0], other[0]) - matmul_exact(operand[1], other[1])
    imag_part = matmul_exact(operand[0], other[1]) + matmul_exact(operand[1], other[0])
    return jnp.stack([real_part, imag_part])


def adjoint_product(operand, other):
    real_part = transposed_product(operand[0], other[0]) + transposed_product(operand[1], other[1])
    imag_part = transposed_product(operand[0], other[1]) - transposed_product(operand[1], other[0])
    return jnp.stack([real_part, imag_part])


def adjoint(operand):
    return jnp.stack([operand[0].T, -operand[1].T])


def real_form(matrix):
    return jnp.block([[matrix[0], -matrix[1]], [matrix[1], matrix[0]]])


def solve_stacked(factor_low, stacked):
    forward_part = lax.linalg.triangular_solve(factor_low, stacked, left_side=True, lower=True)
    return lax.linalg.triangular_solve(
        factor_low, forward_part, left_side=True, lower=True, transpose_a=True
    )


def direct_path(bond_factor, tile_mask, potential, injection):
    orbitals = bond_factor.shape[2]
    tile_size = orbitals // tile_mask.shape[2]
    slab_total = lax.axis_size("slab")
    position = lax.axis_index("slab")
    core_total = lax.axis_size("rhs")
    core_index = lax.axis_index("rhs")
    half_cols = orbitals // core_total
    pattern = jnp.repeat(jnp.repeat(tile_mask[0], tile_size, 0), tile_size, 1).astype(
        bond_factor.dtype
    )
    factor = bond_factor[0] * pattern[None]
    bond_matrix = complex_product(factor, adjoint(factor))
    previous = passed_along(bond_matrix, "slab", 1)
    onsite = jnp.stack([jnp.diag(potential[0]), jnp.zeros((orbitals, orbitals), potential.dtype)])
    matrix = onsite + bond_matrix + previous
    coupling_up = jnp.where(position == slab_total - 1, jnp.zeros_like(bond_matrix), -bond_matrix)
    coupling_down = -previous
    sources = injection[0]

    def apply_inverse(block, right_side):
        factor_low = jnp.linalg.cholesky(real_form(block))
        stacked = jnp.concatenate([right_side[0], right_side[1]], 0)
        solved = solve_stacked(factor_low, stacked)
        return jnp.stack([solved[:orbitals], solved[orbitals:]])

    def own_columns(block):
        return lax.dynamic_slice_in_dim(block, core_index * half_cols, half_cols, 2)

    levels = slab_total.bit_length() - 1
    for rank_bit in range(levels):
        stride = 1 << rank_bit
        spikes = apply_inverse(
            matrix,
            jnp.concatenate([own_columns(coupling_up), own_columns(coupling_down), sources], 2),
        )
        spike_up = spikes[:, :, :half_cols]
        spike_down = spikes[:, :, half_cols : 2 * half_cols]
        spike_waves = spikes[:, :, 2 * half_cols :]
        toward_upper = adjoint_product(
            coupling_down, jnp.concatenate([spike_down, spike_up, spike_waves], 2)
        )
        from_upper = passed_along(toward_upper, "slab", -stride)
        cross_part = toward_upper[:, :, half_cols : 2 * half_cols]
        toward_lower = adjoint_product(coupling_up, jnp.concatenate([spike_up, spike_waves], 2))
        outgoing = jnp.concatenate(
            [toward_lower[:, :, :half_cols], cross_part, toward_lower[:, :, half_cols:]], 2
        )
        from_lower = passed_along(outgoing, "slab", stride)
        diag_change = from_upper[:, :, :half_cols] + from_lower[:, :, :half_cols]
        new_up = -from_upper[:, :, half_cols : 2 * half_cols]
        coupling_new = from_lower[:, :, half_cols : 2 * half_cols]
        sources = sources - from_upper[:, :, 2 * half_cols :] - from_lower[:, :, 2 * half_cols :]
        gathered = (
            lax.all_gather(diag_change, "rhs", axis=2, tiled=True),
            lax.all_gather(new_up, "rhs", axis=2, tiled=True),
            lax.all_gather(coupling_new, "rhs", axis=2, tiled=True),
        )
        matrix = matrix - gathered[0]
        coupling_up = gathered[1]
        coupling_down = -adjoint(gathered[2])
    amplitude = apply_inverse(matrix, sources)
    return amplitude[None]


def split(value):
    high = value.astype(BF16)
    low = (value - high.astype(F32)).astype(BF16)
    return high, low


def dot(left, right):
    return jnp.dot(left, right, preferred_element_type=F32)


def dot3(left, right):
    high = dot(left[0], right[0])
    return high + (dot(left[0], right[1]) + dot(left[1], right[0]))


def pair_map(function, pair):
    return function(pair[0]), function(pair[1])


def tree_kernel(
    slabs,
    factor_ref,
    mask_ref,
    potential_ref,
    injection_ref,
    out_ref,
    flag_ref,
    ground,
    links,
    matrix,
    spare,
    waves,
    flag,
    bond_out,
    bond_in,
    corner_out,
    corner_in,
    ground_out,
    ground_in,
    waves_out,
    far_waves_out,
    waves_in,
    link_out,
    link_in,
    far_out,
    terms_in,
    wave_in,
    wave_out,
    back,
    send_sem,
    bond_sem,
    corner_sem,
    ground_sem,
    waves_sem,
    link_sem,
    terms_sem,
    wave_sem,
    wave_send_sem,
    join_send_sem,
    join_sem,
):
    size = factor_ref.shape[2]
    half = size // 2
    cols = injection_ref.shape[2]
    part_cols = cols // PARTS
    part_width = 2 * part_cols
    part_rows = size // PARTS
    tile = size // mask_ref.shape[2]
    position = lax.axis_index("slab")
    core = lax.axis_index("rhs")
    twin = 1 - core
    levels = slabs.bit_length() - 1

    level = jnp.int32(0)
    stride = jnp.int32(1)
    for k in range(1, levels + 1):
        even = jnp.where(position % (1 << k) == 0, 1, 0)
        level = level + even
        stride = stride + even * (1 << (k - 1))
    not_root = position > 0
    inner = level > 0
    inner_left = jnp.logical_and(inner, not_root)
    deep = level > 1
    deep_left = jnp.logical_and(deep, not_root)
    shallow = position % 4 != 0
    has_right = jnp.logical_and(not_root, position + stride < slabs)
    near_is_right = jnp.logical_and(has_right, (position // stride) % 4 == 1)
    near = jnp.where(near_is_right, 1, 0)
    far = 1 - near
    near_target = jnp.where(near_is_right, position + stride, position - stride)
    far_target = jnp.where(near_is_right, position - stride, position + stride)
    near_is_root = near_target == 0
    sends_ground = jnp.logical_and(not_root, jnp.logical_not(near_is_root))
    sends_link = jnp.logical_and(
        has_right, jnp.logical_or((far_target // stride) % 8 == 4, jnp.logical_and(far_target == 0, stride * 4 == slabs))
    )
    sends_bond = (position + 1) % 4 != 0

    def remote(source, target, sent, received, slab_to, core_to):
        return pltpu.make_async_remote_copy(
            src_ref=source,
            dst_ref=target,
            send_sem=sent,
            recv_sem=received,
            device_id=(slab_to, core_to),
            device_id_type=MESH,
        )

    def arrival(block, received):
        return remote(block, block, send_sem.at[1], received, position, twin)

    def join(block, which):
        return remote(block, block, join_send_sem.at[which], join_sem.at[which], position, twin)

    row = lax.broadcasted_iota(jnp.int32, (size, half), 0)
    lane_half = lax.broadcasted_iota(jnp.int32, (size, half), 1)
    column = lane_half + core * half
    square_row = lax.broadcasted_iota(jnp.int32, (size, size), 0)
    square_column = lax.broadcasted_iota(jnp.int32, (size, size), 1)
    own_real = pl.ds(pl.multiple_of(core * half, half), half)
    own_imag = pl.ds(pl.multiple_of(core * half + size, half), half)

    for h in range(2):
        energies = jnp.broadcast_to(potential_ref[:, h * half : (h + 1) * half], (size, half))
        ground[h, 0] = jnp.where(row == lane_half + h * half, energies, 0.0)
        ground[h, 1] = jnp.zeros((size, half), F32)

    barrier = pltpu.get_barrier_semaphore()

    def greet(slab_to, core_to):
        pl.semaphore_signal(barrier, inc=1, device_id=(slab_to, core_to), device_id_type=MESH)

    greet(position, twin)
    for k in range(levels):
        step = 1 << k
        pl.when(jnp.logical_and(level >= k, position + step < slabs))(
            functools.partial(greet, position + step, core)
        )
        pl.when(jnp.logical_and(level >= k, position >= step))(
            functools.partial(greet, position - step, core)
        )

    def turn(value):
        width = value.shape[1] // 2
        return jnp.concatenate([-value[:, width:], value[:, :width]], 1)

    def expand(value):
        return jnp.concatenate([value, turn(value)], 0)

    def adjoint_of(value):
        return jnp.concatenate([value[:, :size].T, -value[:, size:].T], 1)

    def unpack(square):
        turned = square.T
        real = jnp.where(square_row >= square_column, square, turned)
        below = jnp.where(square_row > square_column, -turned, 0.0)
        imag = jnp.where(square_row < square_column, square, below)
        return jnp.concatenate([real, imag], 1)

    def both_halves(block):
        return jnp.concatenate([block[0], block[1]], 1)

    def whole(block):
        return jnp.concatenate([block[0, 0], block[1, 0], block[0, 1], block[1, 1]], 1)

    lane = lax.broadcasted_iota(jnp.int32, (1, 128), 1)
    masked = []
    for plane in range(2):
        rows = []
        for r in range(size // tile):
            blocks = []
            for k in range(size // 128):
                keep = mask_ref[0, r, k * 128 // tile].astype(F32)
                for t in range(1, 128 // tile):
                    other = mask_ref[0, r, k * 128 // tile + t].astype(F32)
                    keep = jnp.where(lane >= t * tile, other, keep)
                piece = factor_ref[0, plane, r * tile : (r + 1) * tile, k * 128 : (k + 1) * 128]
                blocks.append(piece * keep)
            rows.append(jnp.concatenate(blocks, 1))
        masked.append(jnp.concatenate(rows, 0))
    factor = jnp.concatenate(masked, 1)
    bond = dot3(split(factor), pair_map(expand, split(adjoint_of(factor))))
    packed = jnp.where(square_row >= square_column, bond[:, :size], bond[:, size:])
    bond_out[0] = packed[:, :half]
    bond_out[1] = packed[:, half:]

    waves[...] = jnp.concatenate(
        [
            injection_ref[0, plane, p * part_cols : (p + 1) * part_cols]
            for p in range(PARTS)
            for plane in range(2)
        ],
        0,
    ).T
    flag[...] = jnp.zeros_like(flag)

    partners = jnp.int32(1)
    for k in range(levels):
        step = 1 << k
        partners += jnp.where(jnp.logical_and(level >= k, position + step < slabs), 1, 0)
        partners += jnp.where(jnp.logical_and(level >= k, position >= step), 1, 0)
    pl.semaphore_wait(barrier, partners)

    def bond_copy():
        return remote(
            bond_out.at[core], bond_in.at[core], send_sem.at[0], bond_sem.at[0], position + 1, core
        )

    pl.when(sends_bond)(lambda: bond_copy().start())

    @pl.when(shallow)
    def _():
        arrival(bond_in.at[core], bond_sem.at[0]).wait_recv()
        join(bond_in.at[core], 0).start()
        own_bond = unpack(both_halves(bond_out))

        @pl.when(position < slabs - 1)
        def _():
            links[1] = own_bond

        @pl.when(position == slabs - 1)
        def _():
            for h in range(2):
                for plane in range(2):
                    first = plane * size + h * half
                    ground[h, plane] += own_bond[:, first : first + half]
            links[1] = jnp.zeros((size, 2 * size), F32)

        join(bond_in.at[twin], 0).wait_recv()
        links[0] = unpack(both_halves(bond_in))

    def add_terms(k, side):
        arrival(terms_in.at[k, side], terms_sem.at[k, side]).wait_recv()
        ground[core] += terms_in[k, side]

    def add_waves(k, side):
        arrival(waves_in.at[k, side], waves_sem.at[k, side]).wait_recv()
        waves[...] += waves_in[k, side, 0:size]
        flag[...] = jnp.maximum(flag[...], waves_in[k, side, size : size + 8])

    def add_waves_level(k):
        pl.when(not_root)(functools.partial(add_waves, k, 0))
        add_waves(k, 1)

    @pl.loop(0, jnp.maximum(level - 1, 0))
    def _(k):
        pl.when(not_root)(functools.partial(add_terms, k, 0))
        add_terms(k, 1)

    pl.when(inner)(lambda: join(ground.at[core], 5).start())

    def link_arrival(side):
        arrival(link_in.at[side, core], link_sem.at[side]).wait_recv()
        join(link_in.at[side, core], 6 + side).start()

    def link_whole(side):
        join(link_in.at[side, twin], 6 + side).wait_recv()
        links[side] = adjoint_of(whole(link_in.at[side]))

    pl.when(deep_left)(functools.partial(link_arrival, 0))
    pl.when(deep)(functools.partial(link_arrival, 1))
    pl.when(deep_left)(functools.partial(link_whole, 0))
    pl.when(deep)(functools.partial(link_whole, 1))

    @pl.loop(0, jnp.maximum(level - 2, 0))
    def _(k):
        add_waves_level(k)

    @pl.when(jnp.logical_not(not_root))
    def _():
        links[0] = jnp.zeros((size, 2 * size), F32)

    pl.when(inner)(lambda: join(ground.at[twin], 5).wait_recv())
    matrix[...] = whole(ground) + links[0] + links[1]

    def corner_arrival(side):
        arrival(corner_in.at[side, core], corner_sem.at[side]).wait_recv()
        join(corner_in.at[side, core], 1 + side).start()

    def corner_whole(side):
        join(corner_in.at[side, twin], 1 + side).wait_recv()
        term = unpack(both_halves(corner_in.at[side]))
        matrix[...] -= term
        links[side] -= term

    pl.when(inner_left)(functools.partial(corner_arrival, 0))
    pl.when(inner)(functools.partial(corner_arrival, 1))
    pl.when(inner_left)(functools.partial(corner_whole, 0))
    pl.when(inner)(functools.partial(corner_whole, 1))

    wide_row = lax.broadcasted_iota(jnp.int32, (size, 2 * size), 0)
    wide_column = lax.broadcasted_iota(jnp.int32, (size, 2 * size), 1)
    unit = jnp.where(wide_row == wide_column, 1.0, 0.0).astype(F32)
    mean = jnp.sum(matrix[...] * unit, keepdims=True) / size
    scale = 1.0 / mean
    scaled = matrix[...] * scale
    power = unit - scaled
    inverse = unit + power
    power = power.astype(BF16)
    power = dot(power, expand(power)).astype(BF16)
    for k in range(3):
        both = dot(jnp.concatenate([inverse.astype(BF16), power], 0), expand(power))
        inverse = inverse + both[:size]
        power = both[size:].astype(BF16)
    inverse = inverse + dot(inverse.astype(BF16), expand(power))
    inverse_pair = split(inverse)
    residual = unit - dot3(split(scaled), pair_map(expand, inverse_pair))
    inverse = inverse + dot3(inverse_pair, pair_map(expand, split(residual)))
    squared = jnp.sum(residual * residual, keepdims=True)
    bad = jnp.where(squared < RESIDUAL_LIMIT, 0.0, 1.0)
    flag[...] = jnp.maximum(flag[...], jnp.broadcast_to(bad, (8, 128)))
    solver = split(inverse * scale)

    def ground_arrival(side):
        arrival(ground_in.at[side, core], ground_sem.at[side]).wait_recv()
        join(ground_in.at[side, core], 3 + side).start()

    def ground_whole(side):
        join(ground_in.at[side, twin], 3 + side).wait_recv()
        links[side] -= whole(ground_in.at[side])
        ground[core] += ground_in[side, core]

    pl.when(inner_left)(functools.partial(ground_arrival, 0))
    pl.when(inner_left)(functools.partial(ground_arrival, 1))
    pl.when(inner)(lambda: join(ground.at[core], 5).wait_send())
    pl.when(inner_left)(functools.partial(ground_whole, 0))
    pl.when(inner_left)(functools.partial(ground_whole, 1))

    @pl.when(jnp.logical_not(has_right))
    def _():
        links[1] = jnp.zeros((size, 2 * size), F32)
        wave_in[1] = jnp.zeros(wave_in.shape[1:], F32)

    corner_copy = remote(
        corner_out.at[core],
        corner_in.at[far, core],
        send_sem.at[2],
        corner_sem.at[far],
        near_target,
        core,
    )
    ground_copy = remote(
        ground_out, ground_in.at[far, core], send_sem.at[3], ground_sem.at[far], near_target, core
    )
    waves_copy = remote(
        waves_out,
        waves_in.at[level, far],
        send_sem.at[4],
        waves_sem.at[level, far],
        near_target,
        core,
    )
    far_waves_copy = remote(
        far_waves_out,
        waves_in.at[level, near],
        send_sem.at[7],
        waves_sem.at[level, near],
        far_target,
        core,
    )
    far_copy = remote(
        far_out, terms_in.at[level, near], send_sem.at[5], terms_sem.at[level, near], far_target, core
    )
    link_copy = remote(
        link_out, link_in.at[near, core], send_sem.at[6], link_sem.at[near], far_target, core
    )

    def own_half(ref):
        return jnp.concatenate([ref[:, own_real], ref[:, own_imag]], 1)

    def turn_waves(value):
        swapped = jnp.where(
            lane % part_width < part_cols,
            -pltpu.roll(value, 128 - part_cols, 1),
            pltpu.roll(value, part_cols, 1),
        )
        return jnp.concatenate([value, swapped], 0)

    def expand_waves(value):
        high, low = split(value)
        high_wide, low_wide = high.astype(F32), low.astype(F32)
        return turn_waves(high_wide).astype(BF16), turn_waves(low_wide).astype(BF16)

    def pack_part(value):
        packed_part = value[0:part_rows]
        for q in range(1, PARTS):
            shifted = pltpu.roll(value[q * part_rows : (q + 1) * part_rows], q * part_width, 1)
            packed_part = jnp.where(lane >= q * part_width, shifted, packed_part)
        return packed_part

    def unpack_part(value):
        pieces = [value]
        for q in range(1, PARTS):
            pieces.append(pltpu.roll(value, 128 - q * part_width, 1))
        return jnp.concatenate(pieces, 0)

    def solve_waves():
        @pl.loop(jnp.maximum(level - 2, 0), level)
        def _(k):
            add_waves_level(k)

        solved = dot3(solver, expand_waves(waves[...]))
        waves[...] = solved
        return expand_waves(solved)

    @pl.when(jnp.logical_not(not_root))
    def _():
        solve_waves()

    @pl.when(not_root)
    def _():
        near_adjoint = adjoint_of(links[near])
        near_left = split(near_adjoint)
        sources = jnp.concatenate(
            [links[near, :, own_real], ground[core, 0], links[near, :, own_imag], ground[core, 1]], 1
        )
        solved = dot3(solver, pair_map(expand, split(sources)))
        both_terms = dot3(near_left, pair_map(expand, split(solved)))
        corner_out[core] = jnp.where(
            row >= column, both_terms[:, :half], both_terms[:, size : size + half]
        )
        corner_copy.start()
        pl.when(sends_link)(lambda: join(corner_out.at[core], 8).start())

        ground_out[0] = both_terms[:, half:size]
        ground_out[1] = both_terms[:, size + half :]
        pl.when(sends_ground)(lambda: ground_copy.start())

        @pl.when(sends_link)
        def _():
            join(corner_out.at[twin], 8).wait_recv()
            spare[...] = near_adjoint - unpack(both_halves(corner_out))
            link_out[0] = spare[:, own_real] - ground_out[0]
            link_out[1] = spare[:, own_imag] - ground_out[1]
            link_copy.start()

        solved_ground = pair_map(
            expand,
            split(jnp.concatenate([solved[:, half:size], solved[:, size + half :]], 1)),
        )
        far_left = split(adjoint_of(links[far]))

        @pl.when(has_right)
        def _():
            product = dot3(far_left, solved_ground)
            far_out[0] = product[:, :half]
            far_out[1] = product[:, half:]
            far_copy.start()

        solved_waves = solve_waves()
        waves_out[0:size] = dot3(near_left, solved_waves)
        waves_out[size : size + 8] = flag[...]
        waves_copy.start()

        @pl.when(has_right)
        def _():
            far_waves_out[0:size] = dot3(far_left, solved_waves)
            far_waves_out[size : size + 8] = flag[...]
            far_waves_copy.start()

        for side in range(2):
            spike = split(dot3(solver, pair_map(expand, split(links[side]))))
            for part in range(2):
                back[part, :, side * 2 * size : (side + 1) * 2 * size] = spike[part]

    def wave_sends(k, step, p):
        to_right = remote(
            wave_out.at[p], wave_in.at[0, p], wave_send_sem.at[0, p], wave_sem.at[0, p], position + step, core
        )
        to_left = remote(
            wave_out.at[p], wave_in.at[1, p], wave_send_sem.at[1, p], wave_sem.at[1, p], position - step, core
        )
        return to_right, to_left

    def start_waves(k, step, p):
        to_right, to_left = wave_sends(k, step, p)
        to_right.start()
        pl.when(not_root)(lambda: to_left.start())

    def finish_waves(k, step, p):
        to_right, to_left = wave_sends(k, step, p)
        to_right.wait_send()
        pl.when(not_root)(lambda: to_left.wait_send())

    first_step = jnp.where(inner, stride // 2, 1)
    rows_flag = pl.ds(part_rows, 8)
    for p in range(PARTS):
        own = pltpu.roll(waves[...], 128 - p * part_width, 1) if p else waves[...]
        wave_out[p, 0:part_rows] = pack_part(own)

        @pl.when(not_root)
        def _():
            arrival(wave_in.at[0, p], wave_sem.at[0, p]).wait_recv()
            pl.when(has_right)(lambda: arrival(wave_in.at[1, p], wave_sem.at[1, p]).wait_recv())
            sides = [expand_waves(unpack_part(wave_in[side, p, 0:part_rows])) for side in range(2)]
            pair = [jnp.concatenate([sides[0][e], sides[1][e]], 0) for e in range(2)]
            total = dot3((back[0], back[1]), pair)
            wave_out[p, 0:part_rows] += pack_part(total)
            if p == 0:
                flag[...] = jnp.maximum(flag[...], wave_in[0, 0, rows_flag])

        wave_out[p, rows_flag] = flag[...]
        pl.when(inner)(functools.partial(start_waves, level - 1, first_step, p))

    @pl.when(inner)
    def _():
        for p in range(PARTS):
            finish_waves(level - 1, first_step, p)

    @pl.loop(1, level)
    def _(down):
        k = level - 1 - down
        step = jnp.int32(1)
        for m in range(1, levels):
            step = step + jnp.where(k >= m, 1 << (m - 1), 0)
        for p in range(PARTS):
            start_waves(k, step, p)
        for p in range(PARTS):
            finish_waves(k, step, p)

    turned_waves = jnp.concatenate(
        [unpack_part(wave_out[p, 0:part_rows])[:, :part_width] for p in range(PARTS)], 1
    ).T
    for p in range(PARTS):
        for plane in range(2):
            first = p * part_width + plane * part_cols
            out_ref[0, plane, p * part_cols : (p + 1) * part_cols] = turned_waves[first : first + part_cols]
    flag_ref[...] = flag[0:1, 0:1]

    pl.when(sends_bond)(lambda: bond_copy().wait_send())
    pl.when(shallow)(lambda: join(bond_in.at[core], 0).wait_send())
    for side in range(2):
        pl.when(deep_left if side == 0 else deep)(
            lambda: join(link_in.at[side, core], 6 + side).wait_send()
        )
        pl.when(inner_left if side == 0 else inner)(
            lambda: join(corner_in.at[side, core], 1 + side).wait_send()
        )
        pl.when(inner_left)(lambda: join(ground_in.at[side, core], 3 + side).wait_send())

    @pl.when(not_root)
    def _():
        corner_copy.wait_send()
        pl.when(sends_ground)(lambda: ground_copy.wait_send())
        waves_copy.wait_send()

        @pl.when(has_right)
        def _():
            far_copy.wait_send()
            far_waves_copy.wait_send()

    @pl.when(sends_link)
    def _():
        join(corner_out.at[core], 8).wait_send()
        link_copy.wait_send()


def tree_path(slabs, bond_factor, tile_mask, potential, injection):
    size = bond_factor.shape[2]
    half = size // 2
    levels = slabs.bit_length() - 1
    vmem = pl.BlockSpec(memory_space=pltpu.VMEM)
    dma = pltpu.SemaphoreType.DMA
    turned = jnp.swapaxes(injection, 2, 3)
    amplitude, flag = pl.pallas_call(
        functools.partial(tree_kernel, slabs),
        out_shape=(
            jax.ShapeDtypeStruct(turned.shape, F32),
            jax.ShapeDtypeStruct((1, 1), F32),
        ),
        in_specs=[vmem, pl.BlockSpec(memory_space=pltpu.SMEM), vmem, vmem],
        out_specs=(vmem, vmem),
        scratch_shapes=[
            pltpu.VMEM((2, 2, size, half), F32),
            pltpu.VMEM((2, size, 2 * size), F32),
            pltpu.VMEM((size, 2 * size), F32),
            pltpu.VMEM((size, 2 * size), F32),
            pltpu.VMEM((size, 128), F32),
            pltpu.VMEM((8, 128), F32),
            pltpu.VMEM((2, size, half), F32),
            pltpu.VMEM((2, size, half), F32),
            pltpu.VMEM((2, size, half), F32),
            pltpu.VMEM((2, 2, size, half), F32),
            pltpu.VMEM((2, size, half), F32),
            pltpu.VMEM((2, 2, 2, size, half), F32),
            pltpu.VMEM((size + 8, 128), F32),
            pltpu.VMEM((size + 8, 128), F32),
            pltpu.VMEM((levels, 2, size + 8, 128), F32),
            pltpu.VMEM((2, size, half), F32),
            pltpu.VMEM((2, 2, 2, size, half), F32),
            pltpu.VMEM((2, size, half), F32),
            pltpu.VMEM((levels, 2, 2, size, half), F32),
            pltpu.VMEM((2, PARTS, size // PARTS + 8, 128), F32),
            pltpu.VMEM((PARTS, size // PARTS + 8, 128), F32),
            pltpu.VMEM((2, size, 4 * size), BF16),
            dma((8,)),
            dma((1,)),
            dma((2,)),
            dma((2,)),
            dma((levels, 2)),
            dma((2,)),
            dma((levels, 2)),
            dma((2, PARTS)),
            dma((2, PARTS)),
            dma((9,)),
            dma((9,)),
        ],
        compiler_params=pltpu.CompilerParams(
            collective_id=0, has_side_effects=True, vmem_limit_bytes=52 << 20
        ),
        name="tree_reduction",
    )(bond_factor, tile_mask, potential, turned)
    return jnp.swapaxes(amplitude, 2, 3), flag


def per_device(slabs, bond_factor, tile_mask, potential, injection):
    amplitude, flag = tree_path(slabs, bond_factor, tile_mask, potential, injection)
    return lax.cond(
        flag[0, 0] == 0.0,
        lambda *operands: amplitude,
        direct_path,
        bond_factor,
        tile_mask,
        potential,
        injection,
    )


def solution(mesh):
    in_specs = (
        P("slab", None, None, None),
        P("slab", None, None),
        P("slab", None),
        P("slab", None, None, "rhs"),
    )
    out_specs = P("slab", None, None, "rhs")
    return jax.shard_map(
        functools.partial(per_device, mesh.shape["slab"]),
        mesh=mesh,
        in_specs=in_specs,
        out_specs=out_specs,
        check_vma=False,
    )
```
